32 devices in a mesh: dp: 8 (over y, x, core), seq: 4 (over z).
Axes of the slice: x: 2, y: 2, z: 4, core: 2. Of those that a mesh axis runs over, the one named last changes fastest.
Arguments:
- tokens: bfloat16 [8, 1024, 1024], P('dp', 'seq')
- cotangent: bfloat16 [8, 1024, 1024], P('dp', 'seq'), may hold values from -6 to 6
- valid_length: int32 [8], P('dp'), may hold values from 512 to 1024
- segment_ids: int32 [8, 1024], P('dp'), may hold values from 0 to 3, never falling along the last dimension, each value on 1 to 512 neighbouring positions
- piece_starts: int32 [8, 2], P('dp'), may hold values from 0 to 768, as said below
- norm1_gain: bfloat16 [1024], P(('dp', 'seq')), may hold values from 0.5 to 1.5
- norm1_bias: bfloat16 [1024], P(('dp', 'seq')), may hold values from -3 to 3
- qkv_weight: bfloat16 [1024, 3072], P(('dp', 'seq')), may hold values from -0.1875 to 0.1875
- qv_bias: bfloat16 [2048], P(('dp', 'seq')), may hold values from -3 to 3
- out_weight: bfloat16 [1024, 1024], P(('dp', 'seq')), may hold values from -1.5 to 1.5
- out_bias: bfloat16 [1024], P(('dp', 'seq')), may hold values from -3 to 3
- norm2_gain: bfloat16 [1024], P(('dp', 'seq')), may hold values from 0.5 to 1.5
- norm2_bias: bfloat16 [1024], P(('dp', 'seq')), may hold values from -3 to 3
- up_weight: bfloat16 [1024, 4096], P(('dp', 'seq')), may hold values from -0.1875 to 0.1875
- up_bias: bfloat16 [4096], P(('dp', 'seq')), may hold values from -3 to 3
- down_weight: bfloat16 [4096, 1024], P(('dp', 'seq')), may hold values from -0.09375 to 0.09375
- down_bias: bfloat16 [1024], P(('dp', 'seq')), may hold values from -3 to 3
Outputs:
- output: bfloat16 [8, 1024, 1024], P('dp', 'seq')
- tokens_grad: bfloat16 [8, 1024, 1024], P('dp', 'seq')
- grad_norm1_gain: float32 [1024], P(('dp', 'seq'))
- grad_norm1_bias: float32 [1024], P(('dp', 'seq'))
- grad_qkv_weight: float32 [1024, 3072], P(('dp', 'seq'))
- grad_qv_bias: float32 [2048], P(('dp', 'seq'))
- grad_out_weight: float32 [1024, 1024], P(('dp', 'seq'))
- grad_out_bias: float32 [1024], P(('dp', 'seq'))
- grad_norm2_gain: float32 [1024], P(('dp', 'seq'))
- grad_norm2_bias: float32 [1024], P(('dp', 'seq'))
- grad_up_weight: float32 [1024, 4096], P(('dp', 'seq'))
- grad_up_bias: float32 [4096], P(('dp', 'seq'))
- grad_down_weight: float32 [4096, 1024], P(('dp', 'seq'))
- grad_down_bias: float32 [1024], P(('dp', 'seq'))
- residual_rms: float32 [5], replicated
The draws below stay inside these ranges and needn't reach their ends.
Inputs may be any that keep to these rules, and one draw needn't show every extreme that they name: `piece_starts`: piece p of a sequence starts at p * 512 plus an offset of 0 to 256, so pieces lie in order and never intersect.
All inputs are finite; a program needn't handle non-finite values.
Results may differ from the reference program's by a relative error of at most 0.012.
Values may be sent and summed in bfloat16 or wider, within the bound.
No kernel may reach another device: no remote copies, remote signals or barrier semaphores. Data moves between devices by JAX's collectives and lax.ppermute only.
A program may use at most 192 MiB of HBM per device.

```python
import math
import jax
import jax.numpy as jnp
import numpy as np
from jax import lax

D = 1024
HEADS = 16
HEAD_DIM = 64
FF = 4096
PIECE = 256
PIECES = 2
SEQ_LEN = 1024
SEQS_ALL = 8


def draw_tokens(key, part):
    first = jax.random.fold_in(key, 0)
    where_in = jnp.arange(SEQ_LEN, dtype=jnp.float32) / SEQ_LEN
    which_seq = jnp.arange(SEQS_ALL, dtype=jnp.float32) / SEQS_ALL
    row_scale = 0.5 * jnp.exp(jnp.log(3.0) * (where_in[None, :] + which_seq[:, None]))
    values = jax.random.normal(first, (SEQS_ALL, SEQ_LEN, D), jnp.float32) * row_scale[:, :, None]
    return jnp.clip(values, -8.0, 8.0).astype(jnp.bfloat16)


def draw_piece_starts(key, part):
    room = SEQ_LEN // PIECES - PIECE
    offsets = jax.random.randint(key, (SEQS_ALL, PIECES), 0, room + 1, dtype=jnp.int32)
    offsets = offsets.at[0, 0].set(0).at[0, PIECES - 1].set(room)
    base = jnp.arange(PIECES, dtype=jnp.int32) * (SEQ_LEN // PIECES)
    return base[None, :] + offsets


def touch_ends(drawn, own_key, least, top_value):
    spot = [jax.random.randint(jax.random.fold_in(own_key, axis), (), 0, length) for axis, length in enumerate(drawn.shape)]
    longest = drawn.shape.index(max(drawn.shape))
    beside = spot[:longest] + [(spot[longest] + 1) % drawn.shape[longest]] + spot[longest + 1:]
    return drawn.at[tuple(spot)].set(least).at[tuple(beside)].set(top_value)


def levels(stream_key, dims, cuts, smallest, largest):
    factor_of, own = 1.0, jax.random.fold_in(stream_key, 6)
    for dim, shards_of in cuts:
        draws = jnp.exp(jax.random.uniform(jax.random.fold_in(own, dim), (shards_of,), jnp.float32, smallest / len(cuts), largest / len(cuts)))
        factor_of = factor_of * jnp.repeat(draws, dims[dim] // shards_of).reshape([-1 if axis == dim else 1 for axis in range(len(dims))])
    return factor_of


def length_profile(number_of, total, reach, slope):
    portions = [(1 << 20) // math.isqrt(standing ** slope) + 1 for standing in range(2, number_of + 1)]
    spare, counts = total - reach - (number_of - 1), [1] * (number_of - 1)
    while spare > 0:
        free = [i for i in range(number_of - 1) if counts[i] < reach]
        mass, left = sum([portions[i] for i in free]), spare
        for i in free:
            extra = min(reach - counts[i], max(1, left * portions[i] // mass), spare)
            counts[i] = counts[i] + extra
            spare = spare - extra
    return np.array([reach] + counts)


def ragged(rng, amount, total, reach, slope):
    if amount == 2:
        one = jax.random.randint(rng, (), max(1, total - reach), min(reach, total - 1) + 1)
        return jnp.stack([one, total - one])
    lengths = jnp.asarray(length_profile(amount, total, reach, slope), jnp.int32)
    twos = (amount - 1) // 2
    giver, sink = lengths[1:1 + 2 * twos:2], lengths[2:2 + 2 * twos:2]
    room = jnp.minimum(giver - 1, reach - sink)
    moved = jax.random.randint(jax.random.fold_in(rng, 1), (twos,), 0, 1 << 20) % (room + 1)
    lengths = lengths.at[1:1 + 2 * twos:2].set(giver - moved).at[2:2 + 2 * twos:2].set(sink + moved)
    return lengths[jax.random.permutation(jax.random.fold_in(rng, 2), amount)]


def normal_values(stream_key, dims, scale, reach, cuts=(), held_as=jnp.bfloat16):
    drawn = jax.random.normal(stream_key, dims, jnp.float32) * scale
    if len(cuts) > 0:
        drawn = levels(stream_key, dims, cuts, -0.22, 0.18) * drawn
    return jnp.clip(drawn, min=-reach, max=reach).astype(held_as)


def setup_inputs(seed: int = 0) -> dict:
    keys = jax.random.split(jax.random.key(seed), 18)
    tokens = draw_tokens(jax.random.fold_in(keys[17], 71), 0)
    cotangent = normal_values(keys[1], (SEQS_ALL, SEQ_LEN, D), 1.0, 6.0, ((0, 8), (1, 4)))
    valid_length = touch_ends(jax.random.randint(keys[2], (SEQS_ALL,), SEQ_LEN // 2, SEQ_LEN + 1), jax.random.fold_in(keys[2], 1), SEQ_LEN // 2, SEQ_LEN).astype(jnp.int32)
    segment_ids = jax.vmap(lambda own: jnp.searchsorted(jnp.cumsum(ragged(own, 4, SEQ_LEN, SEQ_LEN // 2, 0)), jnp.arange(SEQ_LEN), side="right"))(jax.random.split(keys[3], SEQS_ALL)).reshape((SEQS_ALL, SEQ_LEN)).astype(jnp.int32)
    piece_starts = draw_piece_starts(jax.random.fold_in(keys[17], 71), 0)
    norm1_gain = jnp.clip(1.0 + 0.1 * jax.random.normal(keys[5], (D,), jnp.float32), 0.5, 1.5).astype(jnp.bfloat16)
    norm1_bias = normal_values(keys[6], (D,), 0.3, 3.0, ((0, 32),))
    qkv_weight = normal_values(keys[7], (D, 3 * D), D ** -0.5, 0.1875, ((0, 32),))
    qv_bias = normal_values(keys[8], (2 * D,), 0.3, 3.0, ((0, 32),))
    out_weight = normal_values(keys[9], (D, D), 16 ** -0.5, 1.5, ((0, 32),))
    out_bias = normal_values(keys[10], (D,), 0.3, 3.0, ((0, 32),))
    norm2_gain = jnp.clip(1.0 + 0.1 * jax.random.normal(keys[11], (D,), jnp.float32), 0.5, 1.5).astype(jnp.bfloat16)
    norm2_bias = normal_values(keys[12], (D,), 0.3, 3.0, ((0, 32),))
    up_weight = normal_values(keys[13], (D, FF), D ** -0.5, 0.1875, ((0, 32),))
    up_bias = normal_values(keys[14], (FF,), 0.3, 3.0, ((0, 32),))
    down_weight = normal_values(keys[15], (FF, D), FF ** -0.5, 0.09375, ((0, 32),))
    down_bias = normal_values(keys[16], (D,), 0.3, 3.0, ((0, 32),))
    return {"tokens": tokens, "cotangent": cotangent, "valid_length": valid_length, "segment_ids": segment_ids, "piece_starts": piece_starts, "norm1_gain": norm1_gain, "norm1_bias": norm1_bias, "qkv_weight": qkv_weight, "qv_bias": qv_bias, "out_weight": out_weight, "out_bias": out_bias, "norm2_gain": norm2_gain, "norm2_bias": norm2_bias, "up_weight": up_weight, "up_bias": up_bias, "down_weight": down_weight, "down_bias": down_bias}


@jax.custom_vjp
def low(v):
    return lax.optimization_barrier(v.astype(jnp.bfloat16)).astype(jnp.float32)

@jax.custom_vjp
def low_back(v):
    return v

def low_keep(v):
    return (low(v), None)

def low_pass(kept, grad):
    return (grad,)

def back_keep(v):
    return (v, None)

def back_low(kept, grad):
    return (low(grad),)
low.defvjp(low_keep, low_pass)
low_back.defvjp(back_keep, back_low)
gelu_scale = 0.7978845608028654
gelu_cubic = 0.044715

def layer_norm(rows_in, gain, shift):
    mean_row = lax.optimization_barrier(jnp.mean(rows_in, axis=-1, keepdims=True))
    centered = rows_in - mean_row
    inverse = lax.rsqrt(lax.optimization_barrier(jnp.mean(centered * centered, axis=-1, keepdims=True)) + 1e-05)
    return centered * inverse * gain + shift

def gelu_tanh(values):
    return 0.5 * values * (1.0 + jnp.tanh(gelu_scale * (values + gelu_cubic * values * values * values)))

def product(left, right):
    return jnp.dot(left, right, precision=lax.Precision.HIGHEST)

def allowed_keys(segment, starts, valid):
    where_at = jnp.arange(SEQ_LEN, dtype=jnp.int32)
    inside = (where_at[:, None] >= starts[None, :]) & (where_at[:, None] < starts[None, :] + PIECE)
    labels = jnp.arange(1, PIECES + 1, dtype=jnp.int32)
    piece_id = lax.optimization_barrier(jnp.sum(jnp.where(inside, labels[None, :], 0), axis=1))
    query_at = where_at[:, None]
    key_at = where_at[None, :]
    same_seg = segment[:, None] == segment[None, :]
    together = (piece_id[:, None] == piece_id[None, :]) & (piece_id[:, None] > 0)
    rule_ok = same_seg & ((key_at <= query_at) | together)
    return (key_at < valid) & ((query_at >= valid) | rule_ok)

def forward(tokens, params, allowed, live_rows):
    norm1_gain, norm1_bias, qkv_weight, qv_bias, out_weight, out_bias, norm2_gain, norm2_bias, up_weight, up_bias, down_weight, down_bias = params
    normed_one = low(layer_norm(tokens, norm1_gain, norm1_bias))
    qkv_shift = jnp.concatenate([qv_bias[:D], jnp.zeros((D,), qv_bias.dtype), qv_bias[D:]])
    qkv_rows = low_back(low(product(normed_one, qkv_weight) + qkv_shift))
    queries = qkv_rows[:, :D].reshape(SEQ_LEN, HEADS, HEAD_DIM)
    key_rows = qkv_rows[:, D:2 * D].reshape(SEQ_LEN, HEADS, HEAD_DIM)
    value_rows = qkv_rows[:, 2 * D:].reshape(SEQ_LEN, HEADS, HEAD_DIM)
    scores = low_back(jnp.einsum('qhd,khd->hqk', queries, key_rows, precision=lax.Precision.HIGHEST) * HEAD_DIM ** (-0.5))
    row_top = lax.optimization_barrier(jnp.max(jnp.where(allowed[None], scores, -1e+30), axis=-1, keepdims=True))
    expo = jnp.exp(jnp.where(allowed[None], scores - row_top, -1e+30))
    attn_probs = expo / lax.optimization_barrier(jnp.sum(expo, axis=-1, keepdims=True))
    head_out = jnp.einsum('hqk,khd->qhd', low(attn_probs), value_rows, precision=lax.Precision.HIGHEST)
    attended = low_back(low(head_out.reshape(SEQ_LEN, D)))
    branch = low_back(product(attended, out_weight) + out_bias)
    middle = tokens + branch
    normed_two = low(layer_norm(middle, norm2_gain, norm2_bias))
    hidden = low_back(product(normed_two, up_weight) + up_bias)
    gated_act = low(gelu_tanh(hidden))
    mlp_out = product(gated_act, down_weight) + down_bias
    result = middle + mlp_out
    squares = jnp.stack([jnp.sum(live_rows[:, None] * field * field) for field in (tokens, branch, middle, mlp_out, result)])
    return (result, squares)

def reference(tokens, cotangent, valid_length, segment_ids, piece_starts, norm1_gain, norm1_bias, qkv_weight, qv_bias, out_weight, out_bias, norm2_gain, norm2_bias, up_weight, up_bias, down_weight, down_bias):
    params = tuple((weight.astype(jnp.float32) for weight in (norm1_gain, norm1_bias, qkv_weight, qv_bias, out_weight, out_bias, norm2_gain, norm2_bias, up_weight, up_bias, down_weight, down_bias)))

    def one_sequence(carry, item):
        grad_sums, square_sums = carry
        seq_tokens, seq_cot, valid, segment, starts = item
        allowed = allowed_keys(segment, starts, valid)
        live_rows = (jnp.arange(SEQ_LEN, dtype=jnp.int32) < valid).astype(jnp.float32)

        def run(rows_in, weights):
            return forward(rows_in, weights, allowed, live_rows)
        result, pull, squares = jax.vjp(run, seq_tokens.astype(jnp.float32), params, has_aux=True)
        grad_rows, grad_weights = pull(seq_cot.astype(jnp.float32) * live_rows[:, None])
        grad_sums = jax.tree.map(jnp.add, grad_sums, grad_weights)
        return ((grad_sums, square_sums + squares), (result.astype(jnp.bfloat16), grad_rows.astype(jnp.bfloat16)))
    start = (jax.tree.map(jnp.zeros_like, params), jnp.zeros((5,), jnp.float32))
    (grad_sums, square_sums), (output, tokens_grad) = lax.scan(one_sequence, start, (tokens, cotangent, valid_length, segment_ids, piece_starts))
    live_total = jnp.sum(valid_length).astype(jnp.float32)
    residual_rms = jnp.sqrt(square_sums / (live_total * D))
    return (output, tokens_grad, grad_sums[0], grad_sums[1], grad_sums[2], grad_sums[3], grad_sums[4], grad_sums[5], grad_sums[6], grad_sums[7], grad_sums[8], grad_sums[9], grad_sums[10], grad_sums[11], residual_rms)
```

```python
import jax
import jax.numpy as jnp
from jax import lax
from jax.sharding import PartitionSpec as P

HEAD_DIM = 64
PIECE = 256


gelu_scale = 0.7978845608028654
gelu_cubic = 0.044715


def layer_norm_parts(rows_in, gain, shift):
    mean_row = jnp.mean(rows_in, axis=-1, keepdims=True)
    centered = rows_in - mean_row
    inverse = lax.rsqrt(jnp.mean(centered * centered, axis=-1, keepdims=True) + 1e-05)
    unit_rows = centered * inverse
    return (unit_rows * gain + shift, unit_rows, inverse)


def layer_norm_back(grad_in, unit_rows, inverse, gain):
    scaled = grad_in * gain
    back_rows = inverse * (
        scaled
        - jnp.mean(scaled, axis=-1, keepdims=True)
        - unit_rows * jnp.mean(scaled * unit_rows, axis=-1, keepdims=True)
    )
    return (back_rows, jnp.sum(grad_in * unit_rows, axis=0), jnp.sum(grad_in, axis=0))


def gelu_parts(values):
    tangent = jnp.tanh(gelu_scale * (values + gelu_cubic * values * values * values))
    slope = 0.5 * (1.0 + tangent) + 0.5 * values * (1.0 - tangent * tangent) * gelu_scale * (
        1.0 + 3.0 * gelu_cubic * values * values
    )
    return (0.5 * values * (1.0 + tangent), slope)


def piece_labels(positions, starts):
    inside = (positions[:, :, None] >= starts[:, None, :]) & (
        positions[:, :, None] < starts[:, None, :] + PIECE
    )
    labels = jnp.arange(1, starts.shape[1] + 1, dtype=jnp.int32)
    return jnp.sum(jnp.where(inside, labels[None, None, :], 0), axis=2)


def visible(query_at, key_at, query_seg, key_seg, query_piece, key_piece, valid):
    query_pos = query_at[None, :, None]
    key_pos = key_at[None, None, :]
    limit_len = valid[:, None, None]
    same_seg = query_seg[:, :, None] == key_seg[:, None, :]
    together = (query_piece[:, :, None] == key_piece[:, None, :]) & (query_piece[:, :, None] > 0)
    rule_ok = same_seg & ((key_pos <= query_pos) | together)
    return (key_pos < limit_len) & ((query_pos >= limit_len) | rule_ok)


def split_heads(rows3):
    seq_count, length, model_width = rows3.shape
    return rows3.reshape(seq_count, length, model_width // HEAD_DIM, HEAD_DIM).transpose(2, 0, 1, 3)


def join_heads(stacked):
    head_count, seq_count, length, head_size = stacked.shape
    return stacked.transpose(1, 2, 0, 3).reshape(seq_count, length, head_count * head_size)


def swap(value, axis, bit, size):
    return lax.ppermute(value, axis, [(i, i ^ bit) for i in range(size)])


def far_bits(dp_size):
    bits = [1 << i for i in range(1, dp_size.bit_length() - 1)]
    half = (len(bits) + 1) // 2
    return bits, bits[half:] + bits[:half]


def place(pieces, me):
    first = pieces[0]
    out = jnp.zeros((len(pieces),) + first.shape, first.dtype)
    for k, piece in pieces.items():
        out = lax.dynamic_update_slice_in_dim(out, piece[None], jnp.bitwise_xor(me, k), 0)
    return out


def gather_rows(shard, dp_size, seq_size, dp_at, seq_at):
    rows, cols = shard.shape
    blocks = {0: shard}
    for k in range(1, seq_size):
        blocks[k] = swap(shard, "seq", k, seq_size)
    local = place(blocks, seq_at).reshape(seq_size * rows, cols)
    orders = far_bits(dp_size)
    halves = []
    for side, order in enumerate(orders):
        part = local[:, side * (cols // 2) : (side + 1) * (cols // 2)]
        pieces = {0: part}
        for bit in order + [1]:
            for k in list(pieces):
                pieces[k ^ bit] = swap(pieces[k], "dp", bit, dp_size)
        halves.append(place(pieces, dp_at).reshape(dp_size * seq_size * rows, cols // 2))
    return jnp.concatenate(halves, axis=1)


def split_bit(value, bit, axis_bits, me):
    axis = axis_bits.index(bit)
    mine = jnp.where(jnp.bitwise_and(me, bit) > 0, 1, 0)
    keep = lax.dynamic_index_in_dim(value, mine, axis, keepdims=False)
    send = lax.dynamic_index_in_dim(value, 1 - mine, axis, keepdims=False)
    return keep, send, [b for b in axis_bits if b != bit]


def scatter_rows(full, dp_size, seq_size, dp_at, seq_at, sent=jnp.bfloat16):
    rows, cols = full.shape
    own = rows // (dp_size * seq_size)
    bits = [1 << i for i in reversed(range(dp_size.bit_length() - 1))]
    value = full.reshape([2] * len(bits) + [seq_size * own, cols])
    keep, send, left_bits = split_bit(value, 1, bits, dp_at)
    value = keep + swap(send.astype(sent), "dp", 1, dp_size).astype(jnp.float32)
    halves = []
    for side, order in enumerate(far_bits(dp_size)):
        part = value[..., side * (cols // 2) : (side + 1) * (cols // 2)]
        part_bits = left_bits
        for bit in order:
            keep, send, part_bits = split_bit(part, bit, part_bits, dp_at)
            part = keep + swap(send.astype(sent), "dp", bit, dp_size).astype(jnp.float32)
        halves.append(part)
    part = jnp.concatenate(halves, axis=1).reshape(seq_size, own, cols)
    total = lax.dynamic_index_in_dim(part, seq_at, 0, keepdims=False)
    part = part.astype(sent)
    for k in range(1, seq_size):
        send = lax.dynamic_index_in_dim(part, jnp.bitwise_xor(seq_at, k), 0, keepdims=False)
        total = total + swap(send, "seq", k, seq_size).astype(jnp.float32)
    return total


def sum_all(value, dp_size, seq_size):
    bit = 1
    while bit < dp_size:
        value = value + swap(value, "dp", bit, dp_size)
        bit *= 2
    bit = 1
    while bit < seq_size:
        value = value + swap(value, "seq", bit, seq_size)
        bit *= 2
    return value


def pack_rows(vectors, devices):
    return jnp.concatenate([v.reshape(devices, -1) for v in vectors], axis=1)


def unpack_rows(packed, widths):
    outs, at = [], 0
    for width in widths:
        outs.append(packed[:, at : at + width].reshape(-1))
        at += width
    return outs


def per_device(
    tokens,
    cotangent,
    valid_length,
    segment_ids,
    piece_starts,
    norm1_gain,
    norm1_bias,
    qkv_weight,
    qv_bias,
    out_weight,
    out_bias,
    norm2_gain,
    norm2_bias,
    up_weight,
    up_bias,
    down_weight,
    down_bias,
):
    seq_count, local_len, model_width = tokens.shape
    full_len = segment_ids.shape[1]
    row_count = seq_count * local_len
    score_scale = HEAD_DIM ** (-0.5)
    dp_size, seq_size = lax.axis_size("dp"), lax.axis_size("seq")
    dp_at, seq_at = lax.axis_index("dp"), lax.axis_index("seq")
    offset = seq_at * local_len
    query_at = offset + jnp.arange(local_len, dtype=jnp.int32)
    key_at = jnp.arange(full_len, dtype=jnp.int32)
    all_pieces = piece_labels(key_at[None, :], piece_starts)
    query_seg = lax.dynamic_slice_in_dim(segment_ids, offset, local_len, 1)
    query_piece = lax.dynamic_slice_in_dim(all_pieces, offset, local_len, 1)
    allowed = visible(
        query_at, key_at, query_seg, segment_ids, query_piece, all_pieces, valid_length
    )
    live_rows = (
        (query_at[None, :] < valid_length[:, None]).astype(jnp.float32).reshape(row_count, 1)
    )
    vectors = (norm1_gain, norm1_bias, qv_bias, out_bias, norm2_gain, norm2_bias, up_bias, down_bias)
    widths = [v.shape[0] for v in vectors]
    gather = lambda shard: gather_rows(shard, dp_size, seq_size, dp_at, seq_at)
    scatter = lambda full, **kw: scatter_rows(full, dp_size, seq_size, dp_at, seq_at, **kw)
    packed = gather(pack_rows(vectors, 1))
    gain_one, shift_one, qv_full, out_shift, gain_two, shift_two, up_shift, down_shift = unpack_rows(
        packed, widths
    )
    qkv_full = gather(qkv_weight)
    out_full = gather(out_weight)
    up_full = gather(up_weight)
    down_full = gather(down_weight)
    tokens_f = tokens.reshape(row_count, model_width).astype(jnp.float32)
    normed_one, unit_one, inverse_one = layer_norm_parts(
        tokens_f, gain_one.astype(jnp.float32), shift_one.astype(jnp.float32)
    )
    normed_one = normed_one.astype(jnp.bfloat16)
    qkv_shift = jnp.concatenate(
        [qv_full[:model_width], jnp.zeros((model_width,), jnp.bfloat16), qv_full[model_width:]]
    ).astype(jnp.float32)
    qkv_rows = (
        jnp.dot(normed_one, qkv_full, preferred_element_type=jnp.float32) + qkv_shift
    ).astype(jnp.bfloat16)
    qkv_three = qkv_rows.reshape(seq_count, local_len, 3 * model_width)
    queries = qkv_three[:, :, :model_width]
    kv_all = lax.all_gather(qkv_three[:, :, model_width:], "seq", axis=1, tiled=True)
    query_heads = split_heads(queries)
    key_heads = split_heads(kv_all[:, :, :model_width])
    value_heads = split_heads(kv_all[:, :, model_width:])
    raw = (
        jnp.einsum("hsqd,hskd->hsqk", query_heads, key_heads, preferred_element_type=jnp.float32)
        * score_scale
    )
    row_top = jnp.max(jnp.where(allowed[None], raw, -1e30), axis=-1, keepdims=True)
    expo = jnp.exp(jnp.where(allowed[None], raw - row_top, -1e30))
    row_total = jnp.sum(expo, axis=-1, keepdims=True)
    attn_probs = (expo / row_total).astype(jnp.bfloat16)
    head_out = jnp.einsum(
        "hsqk,hskd->hsqd", attn_probs, value_heads, preferred_element_type=jnp.float32
    )
    head_outs = head_out.astype(jnp.bfloat16)
    lse_all = row_top[..., 0] + jnp.log(row_total[..., 0])
    attended = join_heads(head_outs).reshape(row_count, model_width)
    branch = jnp.dot(attended, out_full, preferred_element_type=jnp.float32) + out_shift.astype(
        jnp.float32
    )
    middle = tokens_f + branch
    normed_two, unit_two, inverse_two = layer_norm_parts(
        middle, gain_two.astype(jnp.float32), shift_two.astype(jnp.float32)
    )
    normed_two = normed_two.astype(jnp.bfloat16)
    hidden = jnp.dot(normed_two, up_full, preferred_element_type=jnp.float32) + up_shift.astype(
        jnp.float32
    )
    gelu_value, gelu_slope = gelu_parts(hidden)
    gated_act = gelu_value.astype(jnp.bfloat16)
    mlp_out = jnp.dot(gated_act, down_full, preferred_element_type=jnp.float32) + down_shift.astype(
        jnp.float32
    )
    result = middle + mlp_out
    output = result.astype(jnp.bfloat16).reshape(seq_count, local_len, model_width)
    squares = jnp.stack(
        [
            jnp.sum(live_rows * field * field)
            for field in (tokens_f, branch, middle, mlp_out, result)
        ]
    )
    counted = jnp.concatenate([squares, jnp.sum(live_rows)[None]])
    counted = sum_all(jnp.pad(counted, (0, 122))[None], dp_size, seq_size)[0]
    square_sums, live_total = counted[:5], counted[5]
    residual_rms = jnp.sqrt(square_sums / (live_total * model_width))
    qkv_back, out_back, up_back, down_back = qkv_full, out_full, up_full, down_full
    gain_one_b, gain_two_b = gain_one, gain_two
    grad_out = cotangent.reshape(row_count, model_width) * live_rows.astype(jnp.bfloat16)
    grad_down_weight = jnp.einsum(
        "rf,rd->fd", gated_act, grad_out, preferred_element_type=jnp.float32
    )
    grad_down_bias = jnp.sum(grad_out.astype(jnp.float32), axis=0)
    grad_gated = jnp.einsum("rd,fd->rf", grad_out, down_back, preferred_element_type=jnp.float32)
    grad_hidden = (grad_gated * gelu_slope).astype(jnp.bfloat16)
    grad_up_weight = jnp.einsum(
        "rd,rf->df", normed_two, grad_hidden, preferred_element_type=jnp.float32
    )
    grad_up_bias = jnp.sum(grad_hidden.astype(jnp.float32), axis=0)
    grad_normed_two = jnp.einsum(
        "rf,df->rd", grad_hidden, up_back, preferred_element_type=jnp.float32
    )
    grad_mid_norm, grad_norm2_gain, grad_norm2_bias = layer_norm_back(
        grad_normed_two, unit_two, inverse_two, gain_two_b.astype(jnp.float32)
    )
    grad_middle = grad_out.astype(jnp.float32) + grad_mid_norm
    up_grad = scatter(grad_up_weight)
    down_grad = scatter(grad_down_weight)
    grad_branch = grad_middle.astype(jnp.bfloat16)
    grad_out_weight = jnp.einsum(
        "rd,re->de", attended, grad_branch, preferred_element_type=jnp.float32
    )
    grad_out_bias = jnp.sum(grad_branch.astype(jnp.float32), axis=0)
    grad_attended = jnp.einsum(
        "re,de->rd", grad_branch, out_back, preferred_element_type=jnp.float32
    ).astype(jnp.bfloat16)
    grad_attended_three = grad_attended.reshape(seq_count, local_len, model_width)
    grad_heads = split_heads(grad_attended_three)
    raw = (
        jnp.einsum("hsqd,hskd->hsqk", query_heads, key_heads, preferred_element_type=jnp.float32)
        * score_scale
    )
    attn_probs = jnp.exp(jnp.where(allowed[None], raw - lse_all[..., None], -1e30))
    grad_probs = jnp.einsum(
        "hsqd,hskd->hsqk", grad_heads, value_heads, preferred_element_type=jnp.float32
    )
    attn_probs, grad_probs = (attn_probs, grad_probs)
    inner_sum = jnp.sum(attn_probs * grad_probs, axis=-1, keepdims=True)
    grad_scores = (attn_probs * (grad_probs - inner_sum)).astype(jnp.bfloat16)
    grad_query = (
        jnp.einsum("hsqk,hskd->hsqd", grad_scores, key_heads, preferred_element_type=jnp.float32)
        * score_scale
    )
    grad_key = (
        jnp.einsum("hsqk,hsqd->hskd", grad_scores, query_heads, preferred_element_type=jnp.float32)
        * score_scale
    )
    grad_value = jnp.einsum(
        "hsqk,hsqd->hskd",
        attn_probs.astype(jnp.bfloat16),
        grad_heads,
        preferred_element_type=jnp.float32,
    )
    partial_kv = jnp.concatenate([join_heads(grad_key), join_heads(grad_value)], axis=-1)
    local_kv = lax.psum_scatter(
        partial_kv.astype(jnp.bfloat16), "seq", scatter_dimension=1, tiled=True
    ).astype(jnp.float32)
    grad_qkv = jnp.concatenate(
        [
            join_heads(grad_query).reshape(row_count, model_width),
            local_kv.reshape(row_count, 2 * model_width),
        ],
        axis=-1,
    ).astype(jnp.bfloat16)
    grad_qkv_weight = jnp.einsum(
        "rd,re->de", normed_one, grad_qkv, preferred_element_type=jnp.float32
    )
    column_sums = jnp.sum(grad_qkv.astype(jnp.float32), axis=0)
    grad_qv_bias = jnp.concatenate([column_sums[:model_width], column_sums[2 * model_width :]])
    grad_normed_one = jnp.einsum(
        "re,de->rd", grad_qkv, qkv_back, preferred_element_type=jnp.float32
    )
    grad_in_norm, grad_norm1_gain, grad_norm1_bias = layer_norm_back(
        grad_normed_one, unit_one, inverse_one, gain_one_b.astype(jnp.float32)
    )
    tokens_grad = (
        (grad_middle + grad_in_norm).astype(jnp.bfloat16).reshape(seq_count, local_len, model_width)
    )
    qkv_grad = scatter(grad_qkv_weight)
    out_grad = scatter(grad_out_weight)
    vector_grads = (
        grad_norm1_gain,
        grad_norm1_bias,
        grad_qv_bias,
        grad_out_bias,
        grad_norm2_gain,
        grad_norm2_bias,
        grad_up_bias,
        grad_down_bias,
    )
    packed_grads = pack_rows(vector_grads, dp_size * seq_size)
    n1g, n1b, qvb, ob, n2g, n2b, ub, db = unpack_rows(
        scatter(packed_grads, sent=jnp.float32), widths
    )
    return (
        output,
        tokens_grad,
        n1g,
        n1b,
        qkv_grad,
        qvb,
        out_grad,
        ob,
        n2g,
        n2b,
        up_grad,
        ub,
        down_grad,
        db,
        residual_rms,
    )


def solution(mesh):
    return jax.shard_map(
        per_device,
        mesh=mesh,
        in_specs=(
            P("dp", "seq", None),
            P("dp", "seq", None),
            P("dp"),
            P("dp", None),
            P("dp", None),
            P(("dp", "seq")),
            P(("dp", "seq")),
            P(("dp", "seq"), None),
            P(("dp", "seq")),
            P(("dp", "seq"), None),
            P(("dp", "seq")),
            P(("dp", "seq")),
            P(("dp", "seq")),
            P(("dp", "seq"), None),
            P(("dp", "seq")),
            P(("dp", "seq"), None),
            P(("dp", "seq")),
        ),
        out_specs=(
            P("dp", "seq", None),
            P("dp", "seq", None),
            P(("dp", "seq")),
            P(("dp", "seq")),
            P(("dp", "seq"), None),
            P(("dp", "seq")),
            P(("dp", "seq"), None),
            P(("dp", "seq")),
            P(("dp", "seq")),
            P(("dp", "seq")),
            P(("dp", "seq"), None),
            P(("dp", "seq")),
            P(("dp", "seq"), None),
            P(("dp", "seq")),
            P(),
        ),
        check_vma=False,
    )
```

```python
import jax
import jax.numpy as jnp
from jax import lax
from jax.experimental import pallas as pl
from jax.experimental.pallas import tpu as pltpu
from jax.sharding import PartitionSpec as P

HEAD_DIM = 64
PIECE = 256


gelu_scale = 0.7978845608028654
gelu_cubic = 0.044715


def layer_norm_parts(rows_in, gain, shift):
    mean_row = jnp.mean(rows_in, axis=-1, keepdims=True)
    centered = rows_in - mean_row
    inverse = lax.rsqrt(jnp.mean(centered * centered, axis=-1, keepdims=True) + 1e-05)
    unit_rows = centered * inverse
    return (unit_rows * gain + shift, unit_rows, inverse)


def layer_norm_back(grad_in, unit_rows, inverse, gain):
    scaled = grad_in * gain
    back_rows = inverse * (
        scaled
        - jnp.mean(scaled, axis=-1, keepdims=True)
        - unit_rows * jnp.mean(scaled * unit_rows, axis=-1, keepdims=True)
    )
    return (back_rows, jnp.sum(grad_in * unit_rows, axis=0), jnp.sum(grad_in, axis=0))


def gelu_parts(values):
    tangent = jnp.tanh(gelu_scale * (values + gelu_cubic * values * values * values))
    slope = 0.5 * (1.0 + tangent) + 0.5 * values * (1.0 - tangent * tangent) * gelu_scale * (
        1.0 + 3.0 * gelu_cubic * values * values
    )
    return (0.5 * values * (1.0 + tangent), slope)


def piece_labels(positions, starts):
    inside = (positions[:, :, None] >= starts[:, None, :]) & (
        positions[:, :, None] < starts[:, None, :] + PIECE
    )
    labels = jnp.arange(1, starts.shape[1] + 1, dtype=jnp.int32)
    return jnp.sum(jnp.where(inside, labels[None, None, :], 0), axis=2)


def visible(query_at, key_at, query_seg, key_seg, query_piece, key_piece, valid):
    query_pos = query_at[None, :, None]
    key_pos = key_at[None, None, :]
    limit_len = valid[:, None, None]
    same_seg = query_seg[:, :, None] == key_seg[:, None, :]
    together = (query_piece[:, :, None] == key_piece[:, None, :]) & (query_piece[:, :, None] > 0)
    rule_ok = same_seg & ((key_pos <= query_pos) | together)
    return (key_pos < limit_len) & ((query_pos >= limit_len) | rule_ok)


def swap(value, axis, bit, size):
    return lax.ppermute(value, axis, [(i, i ^ bit) for i in range(size)])


def doubled(bits):
    order = [0]
    for bit in bits:
        order = order + [at ^ bit for at in order]
    return order


def far_bits(dp_size):
    bits = [1 << i for i in range(1, dp_size.bit_length() - 1)]
    half = (len(bits) + 1) // 2
    return bits, bits[half:] + bits[:half]


def add(left, right):
    return (left.astype(jnp.float32) + right.astype(jnp.float32)).astype(left.dtype)


def by_place(blocks, me):
    out, bit = list(blocks), 1
    while bit < len(out):
        odd = jnp.bitwise_and(me, bit) > 0
        out = [jnp.where(odd, out[i ^ bit], out[i]) for i in range(len(out))]
        bit *= 2
    return out


def pick_columns_body(index_ref, in_ref, out_ref):
    width = out_ref.shape[1] // index_ref.shape[0]
    for i in range(index_ref.shape[0]):
        at = pl.multiple_of(index_ref[i] * width, width)
        out_ref[:, i * width : (i + 1) * width] = in_ref[:, pl.ds(at, width)]


def pick_columns(rows, index, count):
    width = rows.shape[1] // count
    if width % 128:
        parts = [lax.dynamic_slice_in_dim(rows, index[i] * width, width, 1) for i in range(count)]
        return jnp.concatenate(parts, axis=1)
    return pl.pallas_call(
        pick_columns_body,
        out_shape=jax.ShapeDtypeStruct(rows.shape, rows.dtype),
        in_specs=[
            pl.BlockSpec(memory_space=pltpu.SMEM),
            pl.BlockSpec(memory_space=pltpu.VMEM),
        ],
        out_specs=pl.BlockSpec(memory_space=pltpu.VMEM),
        name="pick_columns",
    )(index, rows)


def pick_rows(table, index):
    chosen = index[:, None] == jnp.arange(table.shape[0], dtype=jnp.int32)[None, :]
    return jnp.sum(jnp.where(chosen[:, :, None], table[None], 0.0), axis=1)


def after(value, *earlier):
    return lax.optimization_barrier((value,) + earlier)[0]


def spread(piece, dp_size, split):
    rows = piece.shape[0]
    bits_x, bits_y = far_bits(dp_size)
    order = doubled(bits_x)
    parts = [(piece, bits_x)]
    if split:
        parts = [(piece[: rows // 2], bits_x), (piece[rows // 2 :], bits_y)]
    bufs = [part for part, _ in parts]
    for step in range(len(bits_x)):
        got = [swap(buf, "dp", bits[step], dp_size) for buf, (_, bits) in zip(bufs, parts)]
        bufs = [jnp.concatenate(pair, axis=0) for pair in zip(bufs, got)]
    if split:
        half, order_y = rows // 2, doubled(bits_y)
        slices = []
        for at in order:
            for buf, places in zip(bufs, (order, order_y)):
                i = places.index(at)
                slices.append(buf[i * half : (i + 1) * half])
        own = jnp.concatenate(slices, axis=0)
    else:
        own = bufs[0]
    return own, swap(own, "dp", 1, dp_size)


def collect(own, odd, dp_size, split):
    bits_x, bits_y = far_bits(dp_size)
    order, count = doubled(bits_x), dp_size // 2
    got = [swap(part, "dp", 1, dp_size) for part in odd]
    stacks = [
        (a.reshape(count, -1, a.shape[1]), b.reshape(count, -1, a.shape[1]))
        for a, b in zip(own, got)
    ]
    rows = stacks[0][0].shape[1]

    def taken(which, low, high):
        cols = [
            jnp.concatenate([add(a[i, low:high], b[i, low:high]) for a, b in stacks], axis=1)
            for i in which
        ]
        return jnp.stack(cols)

    plans = [(bits_x, 0, rows)]
    if split:
        plans = [(bits_x, 0, rows // 2), (bits_y, rows // 2, rows)]
    keeps = []
    half = count // 2
    for bits, low, high in plans:
        places = [order.index(at) for at in doubled(bits)]
        keeps.append((taken(places[:half], low, high), taken(places[half:], low, high)))
    for step in reversed(range(len(bits_x))):
        got = [swap(send, "dp", bits[step], dp_size) for (_, send), (bits, _, _) in zip(keeps, plans)]
        if step:
            cut = (1 << step) // 2
            keeps = [
                (add(keep[:cut], new[:cut]), add(keep[cut:], new[cut:]))
                for (keep, _), new in zip(keeps, got)
            ]
        else:
            keeps = [add(keep, new)[0] for (keep, _), new in zip(keeps, got)]
    return jnp.concatenate(keeps, axis=0)


def seq_gather(shard, seq_size, earlier=()):
    out = [shard]
    for k in range(1, seq_size):
        out.append(swap(after(shard, earlier[k]) if earlier else shard, "seq", k, seq_size))
    return out


def seq_sum(piece, seq_size, seq_at):
    rows = piece.shape[0] // seq_size
    cut = lambda k: lax.dynamic_slice_in_dim(piece, jnp.bitwise_xor(seq_at, k) * rows, rows, 0)
    total = cut(0).astype(jnp.float32)
    for k in range(1, seq_size):
        total = total + swap(cut(k), "seq", k, seq_size).astype(jnp.float32)
    return total


def sum_all(value, dp_size, seq_size):
    bit = 1
    while bit < dp_size:
        value = value + swap(value, "dp", bit, dp_size)
        bit *= 2
    bit = 1
    while bit < seq_size:
        value = value + swap(value, "seq", bit, seq_size)
        bit *= 2
    return value


def dot(left, right):
    return jnp.dot(left, right, preferred_element_type=jnp.float32)


def dot_back(grad, weight):
    return jnp.einsum("rn,kn->rk", grad, weight, preferred_element_type=jnp.float32)


def dot_rows(rows, grad):
    return jnp.einsum("rk,rn->kn", rows, grad, preferred_element_type=jnp.float32)


def apply(rows, pair):
    half = rows.shape[1] // 2
    return dot(rows[:, :half], pair[0]) + dot(rows[:, half:], pair[1])


def apply_back(grad, pair, dtype=jnp.float32):
    return jnp.concatenate([dot_back(grad, part).astype(dtype) for part in pair], axis=1)


def weight_grads(rows, grad):
    half = rows.shape[1] // 2
    return [dot_rows(part, grad).astype(jnp.bfloat16) for part in (rows[:, :half], rows[:, half:])]


def heads_of(rows):
    return rows.reshape(rows.shape[0], -1, HEAD_DIM).transpose(1, 0, 2)


def rows_of(stacked):
    return stacked.transpose(1, 0, 2).reshape(stacked.shape[1], -1)


def per_device(
    tokens,
    cotangent,
    valid_length,
    segment_ids,
    piece_starts,
    norm1_gain,
    norm1_bias,
    qkv_weight,
    qv_bias,
    out_weight,
    out_bias,
    norm2_gain,
    norm2_bias,
    up_weight,
    up_bias,
    down_weight,
    down_bias,
):
    f32, bf16 = jnp.float32, jnp.bfloat16
    _, local_len, width = tokens.shape
    score_scale = HEAD_DIM ** (-0.5)
    dp_size, seq_size = lax.axis_size("dp"), lax.axis_size("seq")
    dp_at, seq_at = lax.axis_index("dp"), lax.axis_index("seq")
    devices = dp_size * seq_size
    group = width // seq_size

    half_order = doubled(far_bits(dp_size)[0])
    full = half_order + [at ^ 1 for at in half_order]
    back = [full.index(at) for at in range(dp_size)]
    full_at = jnp.array(full, jnp.int32)
    to_x = jnp.bitwise_xor(dp_at, full_at)
    natural = jnp.arange(dp_size, dtype=jnp.int32)
    place_in_x = lambda block: jnp.sum(
        jnp.where(
            jnp.bitwise_xor(dp_at, block)[:, None] == natural[None, :],
            jnp.array(back, jnp.int32)[None, :],
            0,
        ),
        axis=1,
    )
    from_x = place_in_x(natural)
    per_group = dp_size // seq_size
    in_groups = lambda block: jnp.bitwise_xor(seq_at, block // per_group) * per_group + block % per_group
    groups_to_x = in_groups(to_x)
    x_to_groups = place_in_x(in_groups(natural))

    vectors = (norm1_gain, norm1_bias, qv_bias, out_bias, norm2_gain, norm2_bias, up_bias, down_bias)
    widths = [v.shape[0] for v in vectors]
    rows_one = qkv_weight.shape[0]
    packed = jnp.concatenate(vectors)
    vec_rows = -(-packed.shape[0] // 128)
    vec_block = jnp.pad(packed, (0, rows_one * 128 - packed.shape[0])).reshape(rows_one, 128)
    qkv_split = qkv_weight.reshape(rows_one, 3, seq_size, group)

    def qkv_part(k):
        mine = lax.dynamic_index_in_dim(qkv_split, jnp.bitwise_xor(seq_at, k), 2, keepdims=False)
        return jnp.concatenate([mine.reshape(rows_one, 3 * group), vec_block], axis=1)

    own_x = pick_columns(tokens[0], to_x, dp_size)
    first = [qkv_part(0)] + [swap(qkv_part(k), "seq", k, seq_size) for k in range(1, seq_size)]
    second = seq_gather(jnp.concatenate([out_weight, up_weight], axis=1), seq_size)
    token_blocks = seq_gather(own_x, seq_size, second)
    third = seq_gather(down_weight, seq_size, token_blocks)
    stacked = lambda blocks: jnp.concatenate(by_place(blocks, seq_at), axis=0)
    one_pair = spread(stacked(first), dp_size, False)
    two_pair = spread(stacked(second), dp_size, True)
    down_pair = spread(stacked(third), dp_size, True)
    qkv_pair = [part[:, : 3 * group] for part in one_pair]
    out_pair = [part[:, :width] for part in two_pair]
    up_pair = [part[:, width:] for part in two_pair]

    vec_x = jnp.concatenate([part[:, 3 * group :] for part in one_pair], axis=0).astype(f32)
    vec_x = vec_x.reshape(dp_size, seq_size, rows_one, 128)[:, :, :vec_rows]
    vec_x = vec_x.reshape(dp_size, seq_size, vec_rows * 128)
    vec_n = pick_rows(vec_x.reshape(dp_size, -1), from_x).reshape(vec_x.shape)

    def field(table, which):
        at = sum(widths[:which])
        return table[:, :, at : at + widths[which]].reshape(-1)

    gain_one, shift_one, gain_two, shift_two = [field(vec_x, i) for i in (0, 1, 4, 5)]
    qv_full, out_shift, up_shift, down_shift = [field(vec_n, i) for i in (2, 3, 6, 7)]

    starts = [jnp.bitwise_xor(seq_at, k) * local_len for k in range(seq_size)]
    step = jnp.arange(local_len, dtype=jnp.int32)
    place = jnp.concatenate([at + step for at in starts])
    segments = jnp.concatenate(
        [lax.dynamic_slice_in_dim(segment_ids, at, local_len, 1) for at in starts], axis=1
    )
    pieces = piece_labels(place[None, :], piece_starts)
    allowed = visible(place, place, segments, segments, pieces, pieces, valid_length)
    live_rows = (starts[0] + step < valid_length[0]).astype(f32)[:, None]

    all_x = jnp.concatenate(token_blocks, axis=0).astype(f32)
    normed_one = layer_norm_parts(all_x, gain_one, shift_one)[0].astype(bf16)
    half_bias = qv_full.reshape(2, seq_size, group)
    half_bias = lax.dynamic_index_in_dim(half_bias, seq_at, 1, keepdims=False)
    qkv_shift = jnp.concatenate([half_bias[0], jnp.zeros((group,), f32), half_bias[1]])
    qkv_rows = (apply(normed_one, qkv_pair) + qkv_shift).astype(bf16)
    query_heads, key_heads, value_heads = [
        heads_of(qkv_rows[:, i * group : (i + 1) * group]) for i in range(3)
    ]
    raw = (
        jnp.einsum("hqd,hkd->hqk", query_heads, key_heads, preferred_element_type=f32) * score_scale
    )
    row_top = jnp.max(jnp.where(allowed, raw, -1e30), axis=-1, keepdims=True)
    expo = jnp.exp(jnp.where(allowed, raw - row_top, -1e30))
    row_total = jnp.sum(expo, axis=-1, keepdims=True)
    attn_probs = (expo / row_total).astype(bf16)
    head_out = jnp.einsum("hqk,hkd->hqd", attn_probs, value_heads, preferred_element_type=f32)
    lse_all = row_top + jnp.log(row_total)
    attended_rows = rows_of(head_out.astype(bf16))

    cut_rows = lambda rows, k: rows[k * local_len : (k + 1) * local_len]
    attended = [cut_rows(attended_rows, 0)] + [
        swap(cut_rows(attended_rows, k), "seq", k, seq_size) for k in range(1, seq_size)
    ]
    attended = pick_columns(jnp.concatenate(attended, axis=1), groups_to_x, dp_size)
    branch = apply(attended, out_pair) + out_shift
    tokens_f = tokens[0].astype(f32)
    middle = tokens_f + branch
    middle_x = pick_columns(middle, to_x, dp_size)
    normed_two, unit_two, inverse_two = layer_norm_parts(middle_x, gain_two, shift_two)
    normed_two = normed_two.astype(bf16)
    hidden = pick_columns(apply(normed_two, up_pair) + up_shift, to_x, dp_size)
    gelu_value, gelu_slope = gelu_parts(hidden)
    gated = gelu_value.astype(bf16)
    mlp_out = apply(gated, down_pair) + down_shift
    result = middle + mlp_out
    output = result.astype(bf16)[None]
    squares = jnp.stack(
        [
            jnp.sum(live_rows * entry * entry)
            for entry in (tokens_f, branch, middle, mlp_out, result)
        ]
    )
    counted = jnp.concatenate([squares, jnp.sum(live_rows)[None]])
    counted = sum_all(jnp.pad(counted, (0, 122))[None], dp_size, seq_size)[0]
    residual_rms = jnp.sqrt(counted[:5] / (counted[5] * width))

    grad_out = cotangent[0] * live_rows.astype(bf16)
    down_grads = weight_grads(gated, grad_out)
    down_piece = collect([down_grads[0]], [down_grads[1]], dp_size, True)
    grad_hidden = (apply_back(grad_out, down_pair) * gelu_slope).astype(bf16)
    grad_hidden = pick_columns(grad_hidden, from_x, dp_size)
    up_grads = weight_grads(normed_two, grad_hidden)
    grad_normed_two = apply_back(grad_hidden, up_pair)
    grad_mid_norm, grad_norm2_gain, grad_norm2_bias = layer_norm_back(
        grad_normed_two, unit_two, inverse_two, gain_two
    )
    grad_middle = grad_out.astype(f32) + pick_columns(grad_mid_norm, from_x, dp_size)
    grad_branch = grad_middle.astype(bf16)
    out_grads = weight_grads(attended, grad_branch)
    grad_attended = pick_columns(apply_back(grad_branch, out_pair, bf16), x_to_groups, dp_size)
    two_piece = collect(
        [out_grads[0], up_grads[0]], [out_grads[1], up_grads[1]], dp_size, True
    )
    cut_cols = lambda rows, k: rows[:, k * group : (k + 1) * group]
    grad_heads = heads_of(
        jnp.concatenate(
            [cut_cols(grad_attended, 0)]
            + [swap(cut_cols(grad_attended, k), "seq", k, seq_size) for k in range(1, seq_size)],
            axis=0,
        )
    )
    raw = (
        jnp.einsum("hqd,hkd->hqk", query_heads, key_heads, preferred_element_type=f32) * score_scale
    )
    attn_probs = jnp.exp(jnp.where(allowed, raw - lse_all, -1e30))
    grad_probs = jnp.einsum("hqd,hkd->hqk", grad_heads, value_heads, preferred_element_type=f32)
    inner_sum = jnp.sum(attn_probs * grad_probs, axis=-1, keepdims=True)
    grad_scores = (attn_probs * (grad_probs - inner_sum)).astype(bf16)
    grad_query = (
        jnp.einsum("hqk,hkd->hqd", grad_scores, key_heads, preferred_element_type=f32) * score_scale
    )
    grad_key = (
        jnp.einsum("hqk,hqd->hkd", grad_scores, query_heads, preferred_element_type=f32)
        * score_scale
    )
    grad_value = jnp.einsum(
        "hqk,hqd->hkd", attn_probs.astype(bf16), grad_heads, preferred_element_type=f32
    )
    grad_qkv = jnp.concatenate(
        [rows_of(part.astype(bf16)) for part in (grad_query, grad_key, grad_value)], axis=1
    )
    part_normed = apply_back(grad_qkv, qkv_pair, bf16)
    grad_normed_one = cut_rows(part_normed, 0).astype(f32)
    for k in range(1, seq_size):
        grad_normed_one = grad_normed_one + swap(
            cut_rows(part_normed, k), "seq", k, seq_size
        ).astype(f32)
    unit_one, inverse_one = layer_norm_parts(own_x.astype(f32), gain_one, shift_one)[1:]
    grad_in_norm, grad_norm1_gain, grad_norm1_bias = layer_norm_back(
        grad_normed_one, unit_one, inverse_one, gain_one
    )
    tokens_grad = (grad_middle + pick_columns(grad_in_norm, from_x, dp_size)).astype(bf16)[None]

    column_sums = jnp.sum(grad_qkv.astype(f32), axis=0).reshape(3, 1, group)
    grad_qv_bias = lax.dynamic_update_slice(
        jnp.zeros((2, seq_size, group), f32),
        jnp.concatenate([column_sums[:1], column_sums[2:]], axis=0),
        (0, seq_at, 0),
    )
    grad_out_bias = jnp.sum(grad_branch.astype(f32), axis=0)
    grad_up_bias = jnp.sum(grad_hidden.astype(f32), axis=0)
    grad_down_bias = jnp.sum(grad_out.astype(f32), axis=0)
    by_device = lambda v: v.reshape(dp_size, seq_size, -1)
    plain = [by_device(v) for v in (grad_qv_bias, grad_out_bias, grad_up_bias, grad_down_bias)]
    plain_widths = [v.shape[2] for v in plain]
    plain_x = pick_rows(jnp.concatenate(plain, axis=2).reshape(dp_size, -1), to_x)
    plain_x = plain_x.reshape(dp_size, seq_size, -1)
    cuts, at = [], 0
    for size in plain_widths:
        cuts.append(plain_x[:, :, at : at + size])
        at += size
    moved = [by_device(v) for v in (grad_norm1_gain, grad_norm1_bias, grad_norm2_gain, grad_norm2_bias)]
    vec_grads = jnp.concatenate(
        [moved[0], moved[1], cuts[0], cuts[1], moved[2], moved[3], cuts[2], cuts[3]], axis=2
    ).astype(bf16)
    vec_size = vec_grads.shape[2]
    vec_grads = jnp.pad(vec_grads, ((0, 0), (0, 0), (0, rows_one * 128 - vec_size)))
    vec_grads = vec_grads.reshape(2, -1, 128)
    qkv_grads = weight_grads(normed_one, grad_qkv)
    one_piece = collect(
        [qkv_grads[0], vec_grads[0]], [qkv_grads[1], vec_grads[1]], dp_size, False
    )
    cut_one = lambda k: lax.dynamic_slice_in_dim(
        one_piece, jnp.bitwise_xor(seq_at, k) * rows_one, rows_one, 0
    )
    one_blocks = [cut_one(0)] + [swap(cut_one(k), "seq", k, seq_size) for k in range(1, seq_size)]
    one_blocks = [block.astype(f32) for block in one_blocks]
    qkv_grad = jnp.stack(
        [part.reshape(rows_one, 3, group) for part in by_place([b[:, : 3 * group] for b in one_blocks], seq_at)],
        axis=2,
    ).reshape(rows_one, 3 * width)
    vec_sum = sum(block[:, 3 * group :] for block in one_blocks).reshape(-1)
    small, at = [], 0
    for size in widths:
        small.append(vec_sum[at : at + size])
        at += size
    n1g, n1b, qvb, ob, n2g, n2b, ub, db = small

    down_grad = seq_sum(down_piece, seq_size, seq_at)
    two_grad = seq_sum(two_piece, seq_size, seq_at)
    out_grad, up_grad = two_grad[:, :width], two_grad[:, width:]
    return (
        output,
        tokens_grad,
        n1g,
        n1b,
        qkv_grad,
        qvb,
        out_grad,
        ob,
        n2g,
        n2b,
        up_grad,
        ub,
        down_grad,
        db,
        residual_rms,
    )


def solution(mesh):
    return jax.shard_map(
        per_device,
        mesh=mesh,
        in_specs=(
            P("dp", "seq", None),
            P("dp", "seq", None),
            P("dp"),
            P("dp", None),
            P("dp", None),
            P(("dp", "seq")),
            P(("dp", "seq")),
            P(("dp", "seq"), None),
            P(("dp", "seq")),
            P(("dp", "seq"), None),
            P(("dp", "seq")),
            P(("dp", "seq")),
            P(("dp", "seq")),
            P(("dp", "seq"), None),
            P(("dp", "seq")),
            P(("dp", "seq"), None),
            P(("dp", "seq")),
        ),
        out_specs=(
            P("dp", "seq", None),
            P("dp", "seq", None),
            P(("dp", "seq")),
            P(("dp", "seq")),
            P(("dp", "seq"), None),
            P(("dp", "seq")),
            P(("dp", "seq"), None),
            P(("dp", "seq")),
            P(("dp", "seq")),
            P(("dp", "seq")),
            P(("dp", "seq"), None),
            P(("dp", "seq")),
            P(("dp", "seq"), None),
            P(("dp", "seq")),
            P(),
        ),
        check_vma=False,
    )
```

```python
import functools

import jax
import jax.numpy as jnp
from jax import lax
from jax.experimental import pallas as pl
from jax.experimental.pallas import tpu as pltpu
from jax.sharding import PartitionSpec as P

HEAD_DIM = 64
PIECE = 256


gelu_scale = 0.7978845608028654
gelu_cubic = 0.044715


def layer_norm_parts(rows_in, gain, shift):
    mean_row = jnp.mean(rows_in, axis=-1, keepdims=True)
    centered = rows_in - mean_row
    inverse = lax.rsqrt(jnp.mean(centered * centered, axis=-1, keepdims=True) + 1e-05)
    unit_rows = centered * inverse
    return (unit_rows * gain + shift, unit_rows, inverse)


def layer_norm_back(grad_in, unit_rows, inverse, gain):
    scaled = grad_in * gain
    back_rows = inverse * (
        scaled
        - jnp.mean(scaled, axis=-1, keepdims=True)
        - unit_rows * jnp.mean(scaled * unit_rows, axis=-1, keepdims=True)
    )
    return (back_rows, jnp.sum(grad_in * unit_rows, axis=0), jnp.sum(grad_in, axis=0))


def gelu_parts(values):
    tangent = jnp.tanh(gelu_scale * (values + gelu_cubic * values * values * values))
    slope = 0.5 * (1.0 + tangent) + 0.5 * values * (1.0 - tangent * tangent) * gelu_scale * (
        1.0 + 3.0 * gelu_cubic * values * values
    )
    return (0.5 * values * (1.0 + tangent), slope)


def piece_labels(positions, starts):
    inside = (positions[:, :, None] >= starts[:, None, :]) & (
        positions[:, :, None] < starts[:, None, :] + PIECE
    )
    labels = jnp.arange(1, starts.shape[1] + 1, dtype=jnp.int32)
    return jnp.sum(jnp.where(inside, labels[None, None, :], 0), axis=2)


def swap(value, axis, bit, size):
    return lax.ppermute(value, axis, [(i, i ^ bit) for i in range(size)])


def doubled(bits):
    order = [0]
    for bit in bits:
        order = order + [at ^ bit for at in order]
    return order


def far_bits(dp_size):
    bits = [1 << i for i in range(1, dp_size.bit_length() - 1)]
    half = (len(bits) + 1) // 2
    return bits, bits[half:] + bits[:half]


def add(left, right):
    return (left.astype(jnp.float32) + right.astype(jnp.float32)).astype(left.dtype)


def by_place(blocks, me):
    out, bit = list(blocks), 1
    while bit < len(out):
        odd = jnp.bitwise_and(me, bit) > 0
        out = [jnp.where(odd, out[i ^ bit], out[i]) for i in range(len(out))]
        bit *= 2
    return out


def pick_columns_body(table, flip_ref, in_ref, out_ref):
    width = out_ref.shape[1] // len(table)
    for i, entry in enumerate(table):
        at = pl.multiple_of(jnp.bitwise_xor(flip_ref[0], entry) * width, width)
        out_ref[:, i * width : (i + 1) * width] = in_ref[:, pl.ds(at, width)]


def pick_columns(rows, table, flip):
    width = rows.shape[1] // len(table)
    if width % 128:
        parts = [
            lax.dynamic_slice_in_dim(rows, jnp.bitwise_xor(flip, entry) * width, width, 1)
            for entry in table
        ]
        return jnp.concatenate(parts, axis=1)
    return pl.pallas_call(
        functools.partial(pick_columns_body, table),
        out_shape=jax.ShapeDtypeStruct(rows.shape, rows.dtype),
        in_specs=[
            pl.BlockSpec(memory_space=pltpu.SMEM),
            pl.BlockSpec(memory_space=pltpu.VMEM),
        ],
        out_specs=pl.BlockSpec(memory_space=pltpu.VMEM),
        name="pick_columns",
    )(flip.reshape(1), rows)


def pick_rows(table, index):
    chosen = index[:, None] == jnp.arange(table.shape[0], dtype=jnp.int32)[None, :]
    return jnp.sum(jnp.where(chosen[:, :, None], table[None], 0.0), axis=1)


def held(value, beside):
    out = lax.optimization_barrier((value,) + tuple(beside))
    return out[0], out[1:]


def place_rows_body(plan, *refs):
    ins, out, held_ref, sems = refs[:-3], refs[-3], refs[-2], refs[-1]
    copies_in, copies_out = [], []
    for i, (source, low, rows, high) in enumerate(plan):
        middle = held_ref.at[high : high + rows, :]
        copies_in.append(
            pltpu.make_async_copy(ins[source].at[low : low + rows, :], middle, sems.at[0, i])
        )
        copies_out.append(
            pltpu.make_async_copy(middle, out.at[high : high + rows, :], sems.at[1, i])
        )
    for copy in copies_in:
        copy.start()
    for copy_in, copy_out in zip(copies_in, copies_out):
        copy_in.wait()
        copy_out.start()
    for copy in copies_out:
        copy.wait()


def place_rows(parts, plan):
    rows, cols = sum(entry[2] for entry in plan), parts[0].shape[1]
    size = rows * cols * parts[0].dtype.itemsize
    return pl.pallas_call(
        functools.partial(place_rows_body, plan),
        out_shape=jax.ShapeDtypeStruct((rows, cols), parts[0].dtype),
        in_specs=[pl.BlockSpec(memory_space=pl.ANY)] * len(parts),
        out_specs=pl.BlockSpec(memory_space=pl.ANY),
        scratch_shapes=[
            pltpu.VMEM((rows, cols), parts[0].dtype),
            pltpu.SemaphoreType.DMA((2, len(plan))),
        ],
        cost_estimate=pl.CostEstimate(flops=0, transcendentals=0, bytes_accessed=2 * size),
        name="place_rows",
    )(*parts)


def spread(piece, dp_size, split):
    rows = piece.shape[0]
    bits_x, bits_y = far_bits(dp_size)
    order = doubled(bits_x)
    parts, plans = (piece,), (bits_x,)
    if split:
        parts, plans = (piece[: rows // 2], piece[rows // 2 :]), (bits_x, bits_y)
    for step in range(len(bits_x)):
        parts = yield tuple(parts)
        got = [swap(part, "dp", bits[step], dp_size) for part, bits in zip(parts, plans)]
        if step + 1 < len(bits_x):
            parts = [jnp.concatenate(pair, axis=0) for pair in zip(parts, got)]
    got = yield tuple(got)
    if split:
        half, order_y, plan = rows // 2, doubled(bits_y), []
        count = len(order) // 2
        for i, at in enumerate(order):
            for side, places in enumerate((order, order_y)):
                j = places.index(at)
                source = side if j < count else 2 + side
                plan.append((source, (j % count) * half, half, (2 * i + side) * half))
        own = place_rows(list(parts) + list(got), plan)
    else:
        own = jnp.concatenate([parts[0], got[0]], axis=0)
    (own,) = yield (own,)
    yield own, swap(own, "dp", 1, dp_size)


def run(stages, values, count):
    for _ in range(count):
        values = stages.send(values)
    return values


def collect(own, odd, dp_size, split):
    bits_x, bits_y = far_bits(dp_size)
    order, count = doubled(bits_x), dp_size // 2
    odd = yield tuple(odd)
    got = [swap(part, "dp", 1, dp_size) for part in odd]
    stacks = [
        (a.reshape(count, -1, a.shape[1]), b.reshape(count, -1, a.shape[1]))
        for a, b in zip(own, got)
    ]
    rows = stacks[0][0].shape[1]

    def taken(which, low, high):
        cols = [
            jnp.concatenate([add(a[i, low:high], b[i, low:high]) for a, b in stacks], axis=1)
            for i in which
        ]
        return jnp.stack(cols)

    plans = [(bits_x, 0, rows)]
    if split:
        plans = [(bits_x, 0, rows // 2), (bits_y, rows // 2, rows)]
    keeps, sends = [], []
    half = count // 2
    for bits, low, high in plans:
        places = [order.index(at) for at in doubled(bits)]
        keeps.append(taken(places[:half], low, high))
        sends.append(taken(places[half:], low, high))
    for step in reversed(range(len(bits_x))):
        sends = yield tuple(sends)
        got = [swap(send, "dp", bits[step], dp_size) for send, (bits, _, _) in zip(sends, plans)]
        if step:
            cut = (1 << step) // 2
            sends = [add(keep[cut:], new[cut:]) for keep, new in zip(keeps, got)]
            keeps = [add(keep[:cut], new[:cut]) for keep, new in zip(keeps, got)]
        else:
            keeps = [add(keep, new)[0] for keep, new in zip(keeps, got)]
    yield (jnp.concatenate(keeps, axis=0),)


def seq_gather(shard, seq_size, earlier=None):
    out, earlier = [shard], list(earlier) if earlier else None
    for k in range(1, seq_size):
        sent = shard
        if earlier:
            sent, (earlier[k],) = held(shard, (earlier[k],))
        out.append(swap(sent, "seq", k, seq_size))
    return out, earlier


def seq_cuts(piece, seq_size, seq_at):
    rows = piece.shape[0] // seq_size
    return tuple(
        lax.dynamic_slice_in_dim(piece, jnp.bitwise_xor(seq_at, k) * rows, rows, 0)
        for k in range(seq_size)
    )


def seq_sum(cuts, seq_size):
    total = cuts[0].astype(jnp.float32)
    for k in range(1, seq_size):
        total = total + swap(cuts[k], "seq", k, seq_size).astype(jnp.float32)
    return total


def dot(left, right):
    return jnp.dot(left, right, preferred_element_type=jnp.float32)


def dot_back(grad, weight):
    return jnp.einsum("rn,kn->rk", grad, weight, preferred_element_type=jnp.float32)


def dot_rows(rows, grad):
    return jnp.einsum("rk,rn->kn", rows, grad, preferred_element_type=jnp.float32)


def apply(rows, pair):
    half = rows.shape[1] // 2
    return dot(rows[:, :half], pair[0]) + dot(rows[:, half:], pair[1])


def apply_back(grad, pair, dtype=jnp.float32):
    return jnp.concatenate([dot_back(grad, part).astype(dtype) for part in pair], axis=1)


def weight_grads(rows, grad):
    half = rows.shape[1] // 2
    return [dot_rows(part, grad).astype(jnp.bfloat16) for part in (rows[:, :half], rows[:, half:])]


def seen(valid_ref, query_ref, key_ref):
    valid = valid_ref[0]
    query_at, query_seg, query_piece = (query_ref[:, i : i + 1] for i in range(3))
    key_at, key_seg, key_piece = (key_ref[i : i + 1, :] for i in range(3))
    together = (query_piece == key_piece) & (query_piece > 0)
    rule_ok = (query_seg == key_seg) & ((key_at <= query_at) | together)
    allowed = (key_at < valid) & ((query_at >= valid) | rule_ok)
    return jnp.where(allowed, 0.0, -1e30)


def one_head(rows, head):
    lane = lax.broadcasted_iota(jnp.int32, rows.shape, 1)
    return jnp.where(lane // HEAD_DIM == head, rows, jnp.zeros_like(rows))


def contract(left, right, dims):
    return lax.dot_general(left, right, (dims, ((), ())), preferred_element_type=jnp.float32)


def attend_body(valid_ref, query_ref, key_ref, q_ref, k_ref, v_ref, out_ref, lse_ref):
    hidden_keys = seen(valid_ref, query_ref, key_ref)
    columns = []
    for at in range(0, q_ref.shape[1], 128):
        pair = slice(at, at + 128)
        query, key, value = q_ref[:, pair], k_ref[:, pair], v_ref[:, pair]
        outs = []
        for head in range(128 // HEAD_DIM):
            raw = contract(one_head(query, head), key, ((1,), (1,)))
            raw = raw * HEAD_DIM ** (-0.5) + hidden_keys
            top = jnp.max(raw, axis=-1, keepdims=True)
            expo = jnp.exp(raw - top)
            total = jnp.sum(expo, axis=-1, keepdims=True)
            probs = (expo * (1.0 / total)).astype(jnp.bfloat16)
            outs.append(contract(probs, value, ((1,), (0,))))
            columns.append(top + jnp.log(total))
        lane = lax.broadcasted_iota(jnp.int32, outs[0].shape, 1)
        out_ref[:, pair] = jnp.where(lane < HEAD_DIM, outs[0], outs[1]).astype(out_ref.dtype)
    for i, column in enumerate(columns):
        lse_ref[:, i : i + 1] = column


def attend_back_body(
    valid_ref, query_ref, key_ref, lse_ref, q_ref, k_ref, v_ref, grad_ref, out_ref, sum_ref
):
    step, group = pl.program_id(0), q_ref.shape[1]
    rows = q_ref.shape[0]

    @pl.when(step == 0)
    def _():
        sum_ref[...] = jnp.zeros_like(sum_ref)

    hidden_keys = seen(valid_ref, query_ref, key_ref)
    at_rows = pl.ds(pl.multiple_of(step * rows, rows), rows)
    scale = HEAD_DIM ** (-0.5)
    for at in range(0, group, 128):
        pair = slice(at, at + 128)
        query, key, value, grad = q_ref[:, pair], k_ref[:, pair], v_ref[:, pair], grad_ref[:, pair]
        grad_query = grad_key = grad_value = 0.0
        for head in range(128 // HEAD_DIM):
            column = at // HEAD_DIM + head
            own_query, own_grad = one_head(query, head), one_head(grad, head)
            raw = contract(own_query, key, ((1,), (1,))) * scale + hidden_keys
            probs = jnp.exp(raw - lse_ref[:, column : column + 1])
            grad_probs = contract(own_grad, value, ((1,), (1,)))
            inner = jnp.sum(probs * grad_probs, axis=-1, keepdims=True)
            grad_scores = (probs * (grad_probs - inner)).astype(jnp.bfloat16)
            grad_value += contract(probs.astype(jnp.bfloat16), own_grad, ((0,), (0,)))
            grad_key += contract(grad_scores, own_query, ((0,), (0,)))
            grad_query += contract(grad_scores, one_head(key, head), ((1,), (0,)))
        out_ref[at_rows, pair] = (grad_query * scale).astype(out_ref.dtype)
        sum_ref[:, pair] += grad_key
        sum_ref[:, group + at : group + at + 128] += grad_value

    @pl.when(step == pl.num_programs(0) - 1)
    def _():
        out_ref[:, group : 2 * group] = (sum_ref[:, :group] * scale).astype(out_ref.dtype)
        out_ref[:, 2 * group :] = sum_ref[:, group:].astype(out_ref.dtype)


def attention_specs(length, group, block):
    whole = lambda column: pl.BlockSpec((length, group), lambda i: (0, column))
    return [
        pl.BlockSpec(memory_space=pltpu.SMEM),
        pl.BlockSpec((block, 3), lambda i: (i, 0)),
        pl.BlockSpec((3, length), lambda i: (0, 0)),
    ], [pl.BlockSpec((block, group), lambda i: (i, 0)), whole(1), whole(2)]


def attend(valid, query_info, key_info, qkv_rows, block=256):
    length, group = qkv_rows.shape[0], qkv_rows.shape[1] // 3
    heads = group // HEAD_DIM
    info_specs, qkv_specs = attention_specs(length, group, block)
    work = heads * length * length
    return pl.pallas_call(
        attend_body,
        grid=(length // block,),
        in_specs=info_specs + qkv_specs,
        out_specs=[
            pl.BlockSpec((block, group), lambda i: (i, 0)),
            pl.BlockSpec((block, heads), lambda i: (i, 0)),
        ],
        out_shape=[
            jax.ShapeDtypeStruct((length, group), jnp.bfloat16),
            jax.ShapeDtypeStruct((length, heads), jnp.float32),
        ],
        cost_estimate=pl.CostEstimate(
            flops=16 * work * HEAD_DIM, transcendentals=work, bytes_accessed=32 * length * group
        ),
        name="attend",
    )(valid, query_info, key_info, qkv_rows, qkv_rows, qkv_rows)


def attend_back(valid, query_info, key_info, lse, qkv_rows, grad_rows, block=256):
    length, group = grad_rows.shape
    heads = group // HEAD_DIM
    info_specs, qkv_specs = attention_specs(length, group, block)
    work = heads * length * length
    return pl.pallas_call(
        attend_back_body,
        grid=(length // block,),
        in_specs=info_specs
        + [pl.BlockSpec((block, heads), lambda i: (i, 0))]
        + qkv_specs
        + [pl.BlockSpec((block, group), lambda i: (i, 0))],
        out_specs=pl.BlockSpec((length, 3 * group), lambda i: (0, 0)),
        out_shape=jax.ShapeDtypeStruct((length, 3 * group), jnp.bfloat16),
        scratch_shapes=[pltpu.VMEM((length, 2 * group), jnp.float32)],
        cost_estimate=pl.CostEstimate(
            flops=40 * work * HEAD_DIM, transcendentals=work, bytes_accessed=64 * length * group
        ),
        name="attend_back",
    )(valid, query_info, key_info, lse, qkv_rows, qkv_rows, qkv_rows, grad_rows)


def per_device(
    tokens,
    cotangent,
    valid_length,
    segment_ids,
    piece_starts,
    norm1_gain,
    norm1_bias,
    qkv_weight,
    qv_bias,
    out_weight,
    out_bias,
    norm2_gain,
    norm2_bias,
    up_weight,
    up_bias,
    down_weight,
    down_bias,
):
    f32, bf16 = jnp.float32, jnp.bfloat16
    _, local_len, width = tokens.shape
    dp_size, seq_size = lax.axis_size("dp"), lax.axis_size("seq")
    dp_at, seq_at = lax.axis_index("dp"), lax.axis_index("seq")
    devices = dp_size * seq_size
    group = width // seq_size

    half_order = doubled(far_bits(dp_size)[0])
    full = half_order + [at ^ 1 for at in half_order]
    back = [full.index(at) for at in range(dp_size)]
    place_in_x = lambda block: sum(
        jnp.where(jnp.bitwise_and(block, 1 << i) > 0, back[1 << i], 0)
        for i in range(dp_size.bit_length() - 1)
    )
    to_x, from_x = (full, dp_at), (back, place_in_x(dp_at))
    in_groups = jnp.bitwise_xor(dp_at, seq_at * (dp_size // seq_size))
    groups_to_x, x_to_groups = (full, in_groups), (back, place_in_x(in_groups))
    index_of = lambda rule: jnp.bitwise_xor(jnp.array(rule[0], jnp.int32), rule[1])

    vectors = (norm1_gain, norm1_bias, qv_bias, out_bias, norm2_gain, norm2_bias, up_bias, down_bias)
    widths = [v.shape[0] for v in vectors]
    rows_one = qkv_weight.shape[0]
    slots = len(vectors) + 1
    in_row = -(-slots // rows_one)
    slot = 128 // in_row
    vec_rows = -(-slots // in_row)

    def slotted(parts):
        rows = []
        for at in range(0, len(parts), in_row):
            row = [
                jnp.pad(v, [(0, 0)] * (v.ndim - 1) + [(0, slot - v.shape[-1])])
                for v in parts[at : at + in_row]
            ]
            row = jnp.concatenate(row, axis=-1) if in_row > 1 else row[0]
            rows.append(jnp.pad(row, [(0, 0)] * (row.ndim - 1) + [(0, 128 - row.shape[-1])]))
        rows = jnp.stack(rows, axis=-2)
        return jnp.pad(rows, [(0, 0)] * (rows.ndim - 2) + [(0, rows_one - rows.shape[-2]), (0, 0)])

    def from_slot(table, which):
        row, low = which // in_row, (which % in_row) * slot
        size = widths[which] if which < len(widths) else 6
        return table[..., row, low : low + size]

    vec_block = slotted(vectors)
    qkv_split = qkv_weight.reshape(rows_one, 3, seq_size, group)

    def qkv_part(k):
        mine = lax.dynamic_index_in_dim(qkv_split, jnp.bitwise_xor(seq_at, k), 2, keepdims=False)
        return jnp.concatenate([mine.reshape(rows_one, 3 * group), vec_block], axis=1)

    first = [qkv_part(0)] + [swap(qkv_part(k), "seq", k, seq_size) for k in range(1, seq_size)]
    own_x = pick_columns(tokens[0], *to_x)
    token_blocks, first = seq_gather(own_x, seq_size, first)
    second, token_blocks = seq_gather(
        jnp.concatenate([out_weight, up_weight], axis=1), seq_size, token_blocks
    )
    far = dp_size.bit_length() - 2
    stacked = lambda blocks: jnp.concatenate(by_place(blocks, seq_at), axis=0)
    one_parts = spread(stacked(first), dp_size, False)
    one_pair = run(one_parts, next(one_parts), far + 2)
    qkv_pair = [part[:, : 3 * group] for part in one_pair]

    vec_x = jnp.concatenate([part[:, 3 * group :] for part in one_pair], axis=0).astype(f32)
    vec_x = vec_x.reshape(dp_size, seq_size, rows_one, 128)[:, :, :vec_rows]
    vec_n = pick_rows(vec_x.reshape(dp_size, -1), index_of(from_x)).reshape(vec_x.shape)

    field = lambda table, which: from_slot(table, which).reshape(-1)
    gain_one, shift_one, gain_two, shift_two = [field(vec_x, i) for i in (0, 1, 4, 5)]
    qv_full, out_shift, up_shift, down_shift = [field(vec_n, i) for i in (2, 3, 6, 7)]

    starts = [jnp.bitwise_xor(seq_at, k) * local_len for k in range(seq_size)]
    step = jnp.arange(local_len, dtype=jnp.int32)
    place = jnp.concatenate([at + step for at in starts])
    segments = jnp.concatenate(
        [lax.dynamic_slice_in_dim(segment_ids, at, local_len, 1) for at in starts], axis=1
    )
    pieces = piece_labels(place[None, :], piece_starts)
    key_info = jnp.concatenate([place[None], segments, pieces], axis=0)
    query_info = key_info.T
    live_rows = (starts[0] + step < valid_length[0]).astype(f32)[:, None]

    all_x = jnp.concatenate(token_blocks, axis=0).astype(f32)
    normed_one, unit_all, _ = layer_norm_parts(all_x, gain_one, shift_one)
    normed_one = normed_one.astype(bf16)
    half_bias = qv_full.reshape(2, seq_size, group)
    half_bias = lax.dynamic_index_in_dim(half_bias, seq_at, 1, keepdims=False)
    qkv_shift = jnp.concatenate([half_bias[0], jnp.zeros((group,), f32), half_bias[1]])
    qkv_rows = (apply(normed_one, qkv_pair) + qkv_shift).astype(bf16)
    attended_rows, lse_all = attend(valid_length, query_info, key_info, qkv_rows)
    attended_rows, second = held(attended_rows, second)

    cut_rows = lambda rows, k: rows[k * local_len : (k + 1) * local_len]
    attended = [cut_rows(attended_rows, 0)] + [
        swap(cut_rows(attended_rows, k), "seq", k, seq_size) for k in range(1, seq_size)
    ]
    two_parts = spread(stacked(second), dp_size, True)
    sends = run(two_parts, next(two_parts), far - 1)
    attended, sends = held(jnp.concatenate(attended, axis=1), sends + (down_weight,))
    third, _ = seq_gather(sends[2], seq_size)
    got = two_parts.send(sends[:2])
    third[0], beside = held(third[0], tuple(third[1:]) + got)
    third = third[:1] + list(beside[:-2])
    own, (piece,) = held(two_parts.send(beside[-2:])[0], (stacked(third),))
    two_pair = two_parts.send((own,))
    down_parts = spread(piece, dp_size, True)
    down_sends = run(down_parts, next(down_parts), far - 1)
    out_pair = [part[:, :width] for part in two_pair]
    up_pair = [part[:, width:] for part in two_pair]

    attended = pick_columns(attended, *groups_to_x)
    branch = apply(attended, out_pair) + out_shift
    tokens_f = tokens[0].astype(f32)
    middle = tokens_f + branch
    middle_x = pick_columns(middle, *to_x)
    middle_x, down_sends = held(middle_x, down_sends)
    down_pair = run(down_parts, down_sends, 3)
    normed_two, unit_two, inverse_two = layer_norm_parts(middle_x, gain_two, shift_two)
    normed_two = normed_two.astype(bf16)
    hidden = pick_columns(apply(normed_two, up_pair) + up_shift, *to_x)
    gelu_value, gelu_slope = gelu_parts(hidden)
    gated = gelu_value.astype(bf16)
    mlp_out = apply(gated, down_pair) + down_shift
    result = middle + mlp_out
    output = result.astype(bf16)[None]
    squares = [
        jnp.sum(live_rows * entry * entry)
        for entry in (tokens_f, branch, middle, mlp_out, result)
    ]
    slots_at = jnp.arange(6, dtype=jnp.int32)
    counted = sum(
        jnp.where(slots_at == i, value, 0.0)
        for i, value in enumerate(squares + [jnp.sum(live_rows)])
    )

    grad_out = cotangent[0] * live_rows.astype(bf16)
    down_grads = weight_grads(gated, grad_out)
    down_sum = collect([down_grads[0]], [down_grads[1]], dp_size, True)
    grad_out_later, sends = held(grad_out, next(down_sum))
    down_sends = down_sum.send(sends)
    grad_hidden = (apply_back(grad_out_later, down_pair) * gelu_slope).astype(bf16)
    grad_hidden = pick_columns(grad_hidden, *from_x)
    grad_hidden, down_sends = held(grad_hidden, down_sends)
    down_sends = down_sum.send(down_sends)
    up_grads = weight_grads(normed_two, grad_hidden)
    up_sum = collect([up_grads[0]], [up_grads[1]], dp_size, True)
    grad_hidden_later, sends = held(grad_hidden, next(up_sum))
    up_sends = up_sum.send(sends)
    grad_normed_two = apply_back(grad_hidden_later, up_pair)
    grad_mid_norm, grad_norm2_gain, grad_norm2_bias = layer_norm_back(
        grad_normed_two, unit_two, inverse_two, gain_two
    )
    grad_mid_norm, down_sends = held(pick_columns(grad_mid_norm, *from_x), down_sends)
    down_sends = down_sum.send(down_sends)
    grad_middle = grad_out.astype(f32) + grad_mid_norm
    grad_branch = grad_middle.astype(bf16)
    out_grads = weight_grads(attended, grad_branch)
    grad_attended = pick_columns(apply_back(grad_branch, out_pair, bf16), *x_to_groups)
    cut_cols = lambda rows, k: rows[:, k * group : (k + 1) * group]
    grad_heads = jnp.concatenate(
        [cut_cols(grad_attended, 0)]
        + [swap(cut_cols(grad_attended, k), "seq", k, seq_size) for k in range(1, seq_size)],
        axis=0,
    )
    down_cuts = seq_cuts(run(down_sum, down_sends, far - 2)[0], seq_size, seq_at)
    grad_heads, sends = held(grad_heads, up_sends + down_cuts)
    up_sends = up_sum.send(sends[:2])
    down_grad = seq_sum(sends[2:], seq_size)
    grad_qkv = attend_back(valid_length, query_info, key_info, lse_all, qkv_rows, grad_heads)
    up_sends = run(up_sum, up_sends, far - 2)
    grad_qkv, sends = held(grad_qkv, up_sends + (down_grad,))
    down_grad = sends[2]
    up_cuts = seq_cuts(up_sum.send(sends[:2])[0], seq_size, seq_at)
    part_normed = apply_back(grad_qkv, qkv_pair)
    grad_norm1_gain = jnp.sum(part_normed * unit_all, axis=0)
    grad_norm1_bias = jnp.sum(part_normed, axis=0)
    part_normed, up_cuts = held(part_normed.astype(bf16), up_cuts)
    column_sums = jnp.sum(grad_qkv.astype(f32), axis=0).reshape(3, 1, group)
    grad_qv_bias = lax.dynamic_update_slice(
        jnp.zeros((2, seq_size, group), f32),
        jnp.concatenate([column_sums[:1], column_sums[2:]], axis=0),
        (0, seq_at, 0),
    )
    grad_out_bias = jnp.sum(grad_branch.astype(f32), axis=0)
    grad_up_bias = jnp.sum(grad_hidden.astype(f32), axis=0)
    grad_down_bias = jnp.sum(grad_out.astype(f32), axis=0)
    by_device = lambda v: v.reshape(dp_size, seq_size, -1)
    plain = [by_device(v) for v in (grad_qv_bias, grad_out_bias, grad_up_bias, grad_down_bias)]
    moved = [by_device(v) for v in (grad_norm1_gain, grad_norm1_bias, grad_norm2_gain, grad_norm2_bias)]
    spare = [jnp.zeros((dp_size, seq_size, 1), f32)] * 2
    plain_x = slotted(spare + plain[:2] + spare + plain[2:])
    plain_x = pick_rows(plain_x.reshape(dp_size, -1), index_of(to_x)).reshape(plain_x.shape)
    spare = spare[:1] * 2
    counts = jnp.broadcast_to(counted, (dp_size, seq_size, 6))
    vec_grads = plain_x + slotted(moved[:2] + spare + moved[2:] + spare + [counts])
    vec_grads = vec_grads.astype(bf16).reshape(2, -1, 128)
    qkv_grads = weight_grads(normed_one, grad_qkv)
    one_sum = collect(
        [qkv_grads[0], vec_grads[0], out_grads[0]],
        [qkv_grads[1], vec_grads[1], out_grads[1]],
        dp_size,
        False,
    )
    sends = next(one_sum)
    for _ in range(dp_size.bit_length() - 1):
        sends = one_sum.send(sends)
    one_cuts = seq_cuts(sends[0], seq_size, seq_at)
    parts = [cut_rows(part_normed, 0)]
    parts += [swap(cut_rows(part_normed, k), "seq", k, seq_size) for k in range(1, seq_size)]
    up_blocks = [up_cuts[0]] + [swap(up_cuts[k], "seq", k, seq_size) for k in range(1, seq_size)]
    one_cuts, parts = held(one_cuts[0], one_cuts[1:] + tuple(parts))
    one_cuts, parts = (one_cuts,) + parts[: seq_size - 1], parts[seq_size - 1 :]
    one_blocks = [one_cuts[0]]
    one_blocks += [swap(one_cuts[k], "seq", k, seq_size) for k in range(1, seq_size)]
    grad_normed_one = sum(part.astype(f32) for part in parts)
    unit_one, inverse_one = layer_norm_parts(own_x.astype(f32), gain_one, shift_one)[1:]
    grad_in_norm = layer_norm_back(grad_normed_one, unit_one, inverse_one, gain_one)[0]
    tokens_grad = (grad_middle + pick_columns(grad_in_norm, *from_x)).astype(bf16)[None]
    up_grad = sum(block.astype(f32) for block in up_blocks)
    one_blocks = [block.astype(f32) for block in one_blocks]
    qkv_grad = jnp.stack(
        [part.reshape(rows_one, 3, group) for part in by_place([b[:, : 3 * group] for b in one_blocks], seq_at)],
        axis=2,
    ).reshape(rows_one, 3 * width)
    rest_sum = sum(block[:, 3 * group :] for block in one_blocks)
    vec_sum, out_grad = rest_sum[:, :128], rest_sum[:, 128:]
    n1g, n1b, qvb, ob, n2g, n2b, ub, db, counted = [from_slot(vec_sum, i) for i in range(slots)]
    residual_rms = jnp.sqrt(counted[:5] / (counted[5] * width))

    return (
        output,
        tokens_grad,
        n1g,
        n1b,
        qkv_grad,
        qvb,
        out_grad,
        ob,
        n2g,
        n2b,
        up_grad,
        ub,
        down_grad,
        db,
        residual_rms,
    )


def solution(mesh):
    return jax.shard_map(
        per_device,
        mesh=mesh,
        in_specs=(
            P("dp", "seq", None),
            P("dp", "seq", None),
            P("dp"),
            P("dp", None),
            P("dp", None),
            P(("dp", "seq")),
            P(("dp", "seq")),
            P(("dp", "seq"), None),
            P(("dp", "seq")),
            P(("dp", "seq"), None),
            P(("dp", "seq")),
            P(("dp", "seq")),
            P(("dp", "seq")),
            P(("dp", "seq"), None),
            P(("dp", "seq")),
            P(("dp", "seq"), None),
            P(("dp", "seq")),
        ),
        out_specs=(
            P("dp", "seq", None),
            P("dp", "seq", None),
            P(("dp", "seq")),
            P(("dp", "seq")),
            P(("dp", "seq"), None),
            P(("dp", "seq")),
            P(("dp", "seq"), None),
            P(("dp", "seq")),
            P(("dp", "seq")),
            P(("dp", "seq")),
            P(("dp", "seq"), None),
            P(("dp", "seq")),
            P(("dp", "seq"), None),
            P(("dp", "seq")),
            P(),
        ),
        check_vma=False,
    )
```

```python
import functools

import jax
import jax.numpy as jnp
from jax import lax
from jax.experimental import pallas as pl
from jax.experimental.pallas import tpu as pltpu
from jax.sharding import PartitionSpec as P

HEAD_DIM = 64
PIECE = 256


gelu_scale = 0.7978845608028654
gelu_cubic = 0.044715


def layer_norm_parts(rows_in, gain, shift):
    mean_row = jnp.mean(rows_in, axis=-1, keepdims=True)
    centered = rows_in - mean_row
    inverse = lax.rsqrt(jnp.mean(centered * centered, axis=-1, keepdims=True) + 1e-05)
    unit_rows = centered * inverse
    return (unit_rows * gain + shift, unit_rows, inverse)


def layer_norm_back(grad_in, unit_rows, inverse, gain):
    scaled = grad_in * gain
    back_rows = inverse * (
        scaled
        - jnp.mean(scaled, axis=-1, keepdims=True)
        - unit_rows * jnp.mean(scaled * unit_rows, axis=-1, keepdims=True)
    )
    return (back_rows, jnp.sum(grad_in * unit_rows, axis=0), jnp.sum(grad_in, axis=0))


def gelu_parts(values):
    tangent = jnp.tanh(gelu_scale * (values + gelu_cubic * values * values * values))
    slope = 0.5 * (1.0 + tangent) + 0.5 * values * (1.0 - tangent * tangent) * gelu_scale * (
        1.0 + 3.0 * gelu_cubic * values * values
    )
    return (0.5 * values * (1.0 + tangent), slope)


def piece_labels(positions, starts):
    inside = (positions[:, :, None] >= starts[:, None, :]) & (
        positions[:, :, None] < starts[:, None, :] + PIECE
    )
    labels = jnp.arange(1, starts.shape[1] + 1, dtype=jnp.int32)
    return jnp.sum(jnp.where(inside, labels[None, None, :], 0), axis=2)


def swap(value, axis, bit, size):
    return lax.ppermute(value, axis, [(i, i ^ bit) for i in range(size)])


def doubled(bits):
    order = [0]
    for bit in bits:
        order = order + [at ^ bit for at in order]
    return order


def far_bits(dp_size):
    bits = [1 << i for i in range(1, dp_size.bit_length() - 1)]
    half = (len(bits) + 1) // 2
    return bits, bits[half:] + bits[:half]


def add(left, right):
    return (left.astype(jnp.float32) + right.astype(jnp.float32)).astype(left.dtype)


def by_place(blocks, me):
    out, bit = list(blocks), 1
    while bit < len(out):
        odd = jnp.bitwise_and(me, bit) > 0
        out = [jnp.where(odd, out[i ^ bit], out[i]) for i in range(len(out))]
        bit *= 2
    return out


def pick_columns_body(table, flip_ref, in_ref, out_ref):
    width = out_ref.shape[1] // len(table)
    for i, entry in enumerate(table):
        at = pl.multiple_of(jnp.bitwise_xor(flip_ref[0], entry) * width, width)
        out_ref[:, i * width : (i + 1) * width] = in_ref[:, pl.ds(at, width)]


def pick_columns(rows, table, flip):
    width = rows.shape[1] // len(table)
    if width % 128:
        parts = [
            lax.dynamic_slice_in_dim(rows, jnp.bitwise_xor(flip, entry) * width, width, 1)
            for entry in table
        ]
        return jnp.concatenate(parts, axis=1)
    return pl.pallas_call(
        functools.partial(pick_columns_body, table),
        out_shape=jax.ShapeDtypeStruct(rows.shape, rows.dtype),
        in_specs=[
            pl.BlockSpec(memory_space=pltpu.SMEM),
            pl.BlockSpec(memory_space=pltpu.VMEM),
        ],
        out_specs=pl.BlockSpec(memory_space=pltpu.VMEM),
        name="pick_columns",
    )(flip.reshape(1), rows)


def pick_rows(table, index):
    chosen = index[:, None] == jnp.arange(table.shape[0], dtype=jnp.int32)[None, :]
    return jnp.sum(jnp.where(chosen[:, :, None], table[None], 0.0), axis=1)


def held(value, beside):
    out = lax.optimization_barrier((value,) + tuple(beside))
    return out[0], out[1:]


def place_rows_body(plan, *refs):
    ins, out, held_ref, sems = refs[:-3], refs[-3], refs[-2], refs[-1]
    copies_in, copies_out = [], []
    for i, (source, low, rows, high) in enumerate(plan):
        middle = held_ref.at[high : high + rows, :]
        copies_in.append(
            pltpu.make_async_copy(ins[source].at[low : low + rows, :], middle, sems.at[0, i])
        )
        copies_out.append(
            pltpu.make_async_copy(middle, out.at[high : high + rows, :], sems.at[1, i])
        )
    for copy in copies_in:
        copy.start()
    for copy_in, copy_out in zip(copies_in, copies_out):
        copy_in.wait()
        copy_out.start()
    for copy in copies_out:
        copy.wait()


def place_rows(parts, plan):
    rows, cols = sum(entry[2] for entry in plan), parts[0].shape[1]
    size = rows * cols * parts[0].dtype.itemsize
    return pl.pallas_call(
        functools.partial(place_rows_body, plan),
        out_shape=jax.ShapeDtypeStruct((rows, cols), parts[0].dtype),
        in_specs=[pl.BlockSpec(memory_space=pl.ANY)] * len(parts),
        out_specs=pl.BlockSpec(memory_space=pl.ANY),
        scratch_shapes=[
            pltpu.VMEM((rows, cols), parts[0].dtype),
            pltpu.SemaphoreType.DMA((2, len(plan))),
        ],
        cost_estimate=pl.CostEstimate(flops=0, transcendentals=0, bytes_accessed=2 * size),
        name="place_rows",
    )(*parts)


def spread(piece, dp_size, split):
    rows = piece.shape[0]
    bits_x, bits_y = far_bits(dp_size)
    order = doubled(bits_x)
    parts, plans = (piece,), (bits_x,)
    if split:
        parts, plans = (piece[: rows // 2], piece[rows // 2 :]), (bits_x, bits_y)
    for step in range(len(bits_x)):
        parts = yield tuple(parts)
        got = [swap(part, "dp", bits[step], dp_size) for part, bits in zip(parts, plans)]
        if step + 1 < len(bits_x):
            parts = [jnp.concatenate(pair, axis=0) for pair in zip(parts, got)]
    got = yield tuple(got)
    if split:
        half, order_y, plan = rows // 2, doubled(bits_y), []
        count = len(order) // 2
        for i, at in enumerate(order):
            for side, places in enumerate((order, order_y)):
                j = places.index(at)
                source = side if j < count else 2 + side
                plan.append((source, (j % count) * half, half, (2 * i + side) * half))
        own = place_rows(list(parts) + list(got), plan)
    else:
        own = jnp.concatenate([parts[0], got[0]], axis=0)
    (own,) = yield (own,)
    yield own, swap(own, "dp", 1, dp_size)


def run(stages, values, count):
    for _ in range(count):
        values = stages.send(values)
    return values


def collect(own, odd, dp_size, split):
    bits_x, bits_y = far_bits(dp_size)
    order, count = doubled(bits_x), dp_size // 2
    odd = yield tuple(odd)
    got = [swap(part, "dp", 1, dp_size) for part in odd]
    stacks = [
        (a.reshape(count, -1, a.shape[1]), b.reshape(count, -1, a.shape[1]))
        for a, b in zip(own, got)
    ]
    rows = stacks[0][0].shape[1]

    def taken(which, low, high):
        cols = [
            jnp.concatenate([add(a[i, low:high], b[i, low:high]) for a, b in stacks], axis=1)
            for i in which
        ]
        return jnp.stack(cols)

    plans = [(bits_x, 0, rows)]
    if split:
        plans = [(bits_x, 0, rows // 2), (bits_y, rows // 2, rows)]
    keeps, sends = [], []
    half = count // 2
    for bits, low, high in plans:
        places = [order.index(at) for at in doubled(bits)]
        keeps.append(taken(places[:half], low, high))
        sends.append(taken(places[half:], low, high))
    for step in reversed(range(len(bits_x))):
        sends = yield tuple(sends)
        got = [swap(send, "dp", bits[step], dp_size) for send, (bits, _, _) in zip(sends, plans)]
        if step:
            cut = (1 << step) // 2
            sends = [add(keep[cut:], new[cut:]) for keep, new in zip(keeps, got)]
            keeps = [add(keep[:cut], new[:cut]) for keep, new in zip(keeps, got)]
        else:
            keeps = [add(keep, new)[0] for keep, new in zip(keeps, got)]
    yield (jnp.concatenate(keeps, axis=0),)


def seq_gather(shard, seq_size, earlier=None):
    out, earlier = [shard], list(earlier) if earlier else None
    for k in range(1, seq_size):
        sent = shard
        if earlier:
            sent, (earlier[k],) = held(shard, (earlier[k],))
        out.append(swap(sent, "seq", k, seq_size))
    return out, earlier


def seq_cuts(piece, seq_size, seq_at):
    rows = piece.shape[0] // seq_size
    return tuple(
        lax.dynamic_slice_in_dim(piece, jnp.bitwise_xor(seq_at, k) * rows, rows, 0)
        for k in range(seq_size)
    )


def seq_sum(cuts, seq_size):
    total = cuts[0].astype(jnp.float32)
    for k in range(1, seq_size):
        total = total + swap(cuts[k], "seq", k, seq_size).astype(jnp.float32)
    return total


def dot(left, right):
    return jnp.dot(left, right, preferred_element_type=jnp.float32)


def dot_back(grad, weight):
    return jnp.einsum("rn,kn->rk", grad, weight, preferred_element_type=jnp.float32)


def dot_rows(rows, grad):
    return jnp.einsum("rk,rn->kn", rows, grad, preferred_element_type=jnp.float32)


def apply(rows, pair):
    half = rows.shape[1] // 2
    return dot(rows[:, :half], pair[0]) + dot(rows[:, half:], pair[1])


def apply_back(grad, pair, dtype=jnp.float32):
    return jnp.concatenate([dot_back(grad, part).astype(dtype) for part in pair], axis=1)


def weight_grads(rows, grad):
    half = rows.shape[1] // 2
    return [dot_rows(part, grad).astype(jnp.bfloat16) for part in (rows[:, :half], rows[:, half:])]


def seen(valid_ref, query_ref, key_ref):
    valid = valid_ref[0]
    query_at, query_seg, query_piece = (query_ref[:, i : i + 1] for i in range(3))
    key_at, key_seg, key_piece = (key_ref[i : i + 1, :] for i in range(3))
    together = (query_piece == key_piece) & (query_piece > 0)
    rule_ok = (query_seg == key_seg) & ((key_at <= query_at) | together)
    allowed = (key_at < valid) & ((query_at >= valid) | rule_ok)
    return jnp.where(allowed, 0.0, -1e30)


def one_head(rows, head):
    lane = lax.broadcasted_iota(jnp.int32, rows.shape, 1)
    return jnp.where(lane // HEAD_DIM == head, rows, jnp.zeros_like(rows))


def contract(left, right, dims):
    return lax.dot_general(left, right, (dims, ((), ())), preferred_element_type=jnp.float32)


def attend_body(valid_ref, query_ref, key_ref, q_ref, k_ref, v_ref, out_ref, lse_ref):
    hidden_keys = seen(valid_ref, query_ref, key_ref)
    columns = []
    for at in range(0, q_ref.shape[1], 128):
        pair = slice(at, at + 128)
        query, key, value = q_ref[:, pair], k_ref[:, pair], v_ref[:, pair]
        outs = []
        for head in range(128 // HEAD_DIM):
            raw = contract(one_head(query, head), key, ((1,), (1,)))
            raw = raw * HEAD_DIM ** (-0.5) + hidden_keys
            top = jnp.max(raw, axis=-1, keepdims=True)
            expo = jnp.exp(raw - top)
            total = jnp.sum(expo, axis=-1, keepdims=True)
            probs = (expo * (1.0 / total)).astype(jnp.bfloat16)
            outs.append(contract(probs, value, ((1,), (0,))))
            columns.append(top + jnp.log(total))
        lane = lax.broadcasted_iota(jnp.int32, outs[0].shape, 1)
        out_ref[:, pair] = jnp.where(lane < HEAD_DIM, outs[0], outs[1]).astype(out_ref.dtype)
    for i, column in enumerate(columns):
        lse_ref[:, i : i + 1] = column


def attend_back_body(
    valid_ref, query_ref, key_ref, lse_ref, q_ref, k_ref, v_ref, grad_ref, out_ref, sum_ref
):
    step, group = pl.program_id(0), q_ref.shape[1]
    rows = q_ref.shape[0]

    @pl.when(step == 0)
    def _():
        sum_ref[...] = jnp.zeros_like(sum_ref)

    hidden_keys = seen(valid_ref, query_ref, key_ref)
    at_rows = pl.ds(pl.multiple_of(step * rows, rows), rows)
    scale = HEAD_DIM ** (-0.5)
    for at in range(0, group, 128):
        pair = slice(at, at + 128)
        query, key, value, grad = q_ref[:, pair], k_ref[:, pair], v_ref[:, pair], grad_ref[:, pair]
        grad_query = grad_key = grad_value = 0.0
        for head in range(128 // HEAD_DIM):
            column = at // HEAD_DIM + head
            own_query, own_grad = one_head(query, head), one_head(grad, head)
            raw = contract(own_query, key, ((1,), (1,))) * scale + hidden_keys
            probs = jnp.exp(raw - lse_ref[:, column : column + 1])
            grad_probs = contract(own_grad, value, ((1,), (1,)))
            inner = jnp.sum(probs * grad_probs, axis=-1, keepdims=True)
            grad_scores = (probs * (grad_probs - inner)).astype(jnp.bfloat16)
            grad_value += contract(probs.astype(jnp.bfloat16), own_grad, ((0,), (0,)))
            grad_key += contract(grad_scores, own_query, ((0,), (0,)))
            grad_query += contract(grad_scores, one_head(key, head), ((1,), (0,)))
        out_ref[at_rows, pair] = (grad_query * scale).astype(out_ref.dtype)
        sum_ref[:, pair] += grad_key
        sum_ref[:, group + at : group + at + 128] += grad_value

    @pl.when(step == pl.num_programs(0) - 1)
    def _():
        out_ref[:, group : 2 * group] = (sum_ref[:, :group] * scale).astype(out_ref.dtype)
        out_ref[:, 2 * group :] = sum_ref[:, group:].astype(out_ref.dtype)


def attention_specs(length, group, block):
    whole = lambda column: pl.BlockSpec((length, group), lambda i: (0, column))
    return [
        pl.BlockSpec(memory_space=pltpu.SMEM),
        pl.BlockSpec((block, 3), lambda i: (i, 0)),
        pl.BlockSpec((3, length), lambda i: (0, 0)),
    ], [pl.BlockSpec((block, group), lambda i: (i, 0)), whole(1), whole(2)]


def attend(valid, query_info, key_info, qkv_rows, block=256):
    length, group = qkv_rows.shape[0], qkv_rows.shape[1] // 3
    heads = group // HEAD_DIM
    info_specs, qkv_specs = attention_specs(length, group, block)
    work = heads * length * length
    return pl.pallas_call(
        attend_body,
        grid=(length // block,),
        in_specs=info_specs + qkv_specs,
        out_specs=[
            pl.BlockSpec((block, group), lambda i: (i, 0)),
            pl.BlockSpec((block, heads), lambda i: (i, 0)),
        ],
        out_shape=[
            jax.ShapeDtypeStruct((length, group), jnp.bfloat16),
            jax.ShapeDtypeStruct((length, heads), jnp.float32),
        ],
        cost_estimate=pl.CostEstimate(
            flops=16 * work * HEAD_DIM, transcendentals=work, bytes_accessed=32 * length * group
        ),
        name="attend",
    )(valid, query_info, key_info, qkv_rows, qkv_rows, qkv_rows)


def attend_back(valid, query_info, key_info, lse, qkv_rows, grad_rows, block=256):
    length, group = grad_rows.shape
    heads = group // HEAD_DIM
    info_specs, qkv_specs = attention_specs(length, group, block)
    work = heads * length * length
    return pl.pallas_call(
        attend_back_body,
        grid=(length // block,),
        in_specs=info_specs
        + [pl.BlockSpec((block, heads), lambda i: (i, 0))]
        + qkv_specs
        + [pl.BlockSpec((block, group), lambda i: (i, 0))],
        out_specs=pl.BlockSpec((length, 3 * group), lambda i: (0, 0)),
        out_shape=jax.ShapeDtypeStruct((length, 3 * group), jnp.bfloat16),
        scratch_shapes=[pltpu.VMEM((length, 2 * group), jnp.float32)],
        cost_estimate=pl.CostEstimate(
            flops=40 * work * HEAD_DIM, transcendentals=work, bytes_accessed=64 * length * group
        ),
        name="attend_back",
    )(valid, query_info, key_info, lse, qkv_rows, qkv_rows, qkv_rows, grad_rows)


def per_device(
    tokens,
    cotangent,
    valid_length,
    segment_ids,
    piece_starts,
    norm1_gain,
    norm1_bias,
    qkv_weight,
    qv_bias,
    out_weight,
    out_bias,
    norm2_gain,
    norm2_bias,
    up_weight,
    up_bias,
    down_weight,
    down_bias,
):
    f32, bf16 = jnp.float32, jnp.bfloat16
    _, local_len, width = tokens.shape
    dp_size, seq_size = lax.axis_size("dp"), lax.axis_size("seq")
    dp_at, seq_at = lax.axis_index("dp"), lax.axis_index("seq")
    devices = dp_size * seq_size
    group = width // seq_size

    half_order = doubled(far_bits(dp_size)[0])
    full = half_order + [at ^ 1 for at in half_order]
    back = [full.index(at) for at in range(dp_size)]
    place_in_x = lambda block: sum(
        jnp.where(jnp.bitwise_and(block, 1 << i) > 0, back[1 << i], 0)
        for i in range(dp_size.bit_length() - 1)
    )
    to_x, from_x = (full, dp_at), (back, place_in_x(dp_at))
    in_groups = jnp.bitwise_xor(dp_at, seq_at * (dp_size // seq_size))
    groups_to_x, x_to_groups = (full, in_groups), (back, place_in_x(in_groups))
    index_of = lambda rule: jnp.bitwise_xor(jnp.array(rule[0], jnp.int32), rule[1])

    vectors = (norm1_gain, norm1_bias, qv_bias, out_bias, norm2_gain, norm2_bias, up_bias, down_bias)
    widths = [v.shape[0] for v in vectors]
    rows_one = qkv_weight.shape[0]
    slots = len(vectors) + 1
    in_row = -(-slots // rows_one)
    slot = 128 // in_row
    vec_rows = -(-slots // in_row)

    def slotted(parts):
        rows = []
        for at in range(0, len(parts), in_row):
            row = [
                jnp.pad(v, [(0, 0)] * (v.ndim - 1) + [(0, slot - v.shape[-1])])
                for v in parts[at : at + in_row]
            ]
            row = jnp.concatenate(row, axis=-1) if in_row > 1 else row[0]
            rows.append(jnp.pad(row, [(0, 0)] * (row.ndim - 1) + [(0, 128 - row.shape[-1])]))
        rows = jnp.stack(rows, axis=-2)
        return jnp.pad(rows, [(0, 0)] * (rows.ndim - 2) + [(0, rows_one - rows.shape[-2]), (0, 0)])

    def from_slot(table, which):
        row, low = which // in_row, (which % in_row) * slot
        size = widths[which] if which < len(widths) else 6
        return table[..., row, low : low + size]

    vec_block = slotted(vectors)
    qkv_split = qkv_weight.reshape(rows_one, 3, seq_size, group)

    def qkv_part(k):
        mine = lax.dynamic_index_in_dim(qkv_split, jnp.bitwise_xor(seq_at, k), 2, keepdims=False)
        return jnp.concatenate([mine.reshape(rows_one, 3 * group), vec_block], axis=1)

    first = [qkv_part(0)] + [swap(qkv_part(k), "seq", k, seq_size) for k in range(1, seq_size)]
    own_x = pick_columns(tokens[0], *to_x)
    second, _ = seq_gather(jnp.concatenate([out_weight, up_weight], axis=1), seq_size)
    token_blocks = [own_x]
    for k in range(1, seq_size):
        sent, (first[k], second[k]) = held(own_x, (first[k], second[k]))
        token_blocks.append(swap(sent, "seq", k, seq_size))
    far = dp_size.bit_length() - 2
    stacked = lambda blocks: jnp.concatenate(by_place(blocks, seq_at), axis=0)
    one_parts = spread(stacked(first), dp_size, False)
    one_pair = run(one_parts, next(one_parts), far + 2)
    two_parts = spread(stacked(second), dp_size, True)
    two_sends = run(two_parts, next(two_parts), far - 1)
    token_blocks[0], beside = held(token_blocks[0], tuple(token_blocks[1:]) + two_sends)
    token_blocks = token_blocks[:1] + list(beside[: seq_size - 1])
    got = two_parts.send(beside[seq_size - 1 :])
    third, token_blocks = seq_gather(down_weight, seq_size, token_blocks)
    qkv_pair = [part[:, : 3 * group] for part in one_pair]

    vec_x = jnp.concatenate([part[:, 3 * group :] for part in one_pair], axis=0).astype(f32)
    vec_x = vec_x.reshape(dp_size, seq_size, rows_one, 128)[:, :, :vec_rows]
    vec_n = pick_rows(vec_x.reshape(dp_size, -1), index_of(from_x)).reshape(vec_x.shape)

    field = lambda table, which: from_slot(table, which).reshape(-1)
    gain_one, shift_one, gain_two, shift_two = [field(vec_x, i) for i in (0, 1, 4, 5)]
    qv_full, out_shift, up_shift, down_shift = [field(vec_n, i) for i in (2, 3, 6, 7)]

    starts = [jnp.bitwise_xor(seq_at, k) * local_len for k in range(seq_size)]
    step = jnp.arange(local_len, dtype=jnp.int32)
    place = jnp.concatenate([at + step for at in starts])
    segments = jnp.concatenate(
        [lax.dynamic_slice_in_dim(segment_ids, at, local_len, 1) for at in starts], axis=1
    )
    pieces = piece_labels(place[None, :], piece_starts)
    key_info = jnp.concatenate([place[None], segments, pieces], axis=0)
    query_info = key_info.T
    live_rows = (starts[0] + step < valid_length[0]).astype(f32)[:, None]

    all_x = jnp.concatenate(token_blocks, axis=0).astype(f32)
    normed_one, unit_all, _ = layer_norm_parts(all_x, gain_one, shift_one)
    normed_one = normed_one.astype(bf16)
    half_bias = qv_full.reshape(2, seq_size, group)
    half_bias = lax.dynamic_index_in_dim(half_bias, seq_at, 1, keepdims=False)
    qkv_shift = jnp.concatenate([half_bias[0], jnp.zeros((group,), f32), half_bias[1]])
    qkv_rows = (apply(normed_one, qkv_pair) + qkv_shift).astype(bf16)
    attended_rows, lse_all = attend(valid_length, query_info, key_info, qkv_rows)
    attended_rows, beside = held(attended_rows, tuple(third) + tuple(got))
    third, got = beside[:-2], beside[-2:]
    cut_rows = lambda rows, k: rows[k * local_len : (k + 1) * local_len]
    attended = [cut_rows(attended_rows, 0)] + [
        swap(cut_rows(attended_rows, k), "seq", k, seq_size) for k in range(1, seq_size)
    ]
    own, (piece,) = held(two_parts.send(got)[0], (stacked(third),))
    two_pair = two_parts.send((own,))
    out_pair = [part[:, :width] for part in two_pair]
    up_pair = [part[:, width:] for part in two_pair]
    down_parts = spread(piece, dp_size, True)
    down_sends = run(down_parts, next(down_parts), far - 1)

    attended, down_sends = held(jnp.concatenate(attended, axis=1), down_sends)
    got = down_parts.send(down_sends)
    attended = pick_columns(attended, *groups_to_x)
    branch = apply(attended, out_pair) + out_shift
    tokens_f = tokens[0].astype(f32)
    middle = tokens_f + branch
    middle_x = pick_columns(middle, *to_x)
    normed_two, unit_two, inverse_two = layer_norm_parts(middle_x, gain_two, shift_two)
    normed_two = normed_two.astype(bf16)
    hidden = pick_columns(apply(normed_two, up_pair) + up_shift, *to_x)
    hidden, got = held(hidden, got)
    down_pair = run(down_parts, got, 2)
    gated = gelu_parts(hidden)[0].astype(bf16)
    mlp_out = apply(gated, down_pair) + down_shift
    result = middle + mlp_out
    output = result.astype(bf16)[None]
    squares = [
        jnp.sum(live_rows * entry * entry)
        for entry in (tokens_f, branch, middle, mlp_out, result)
    ]
    slots_at = jnp.arange(6, dtype=jnp.int32)
    counted = sum(
        jnp.where(slots_at == i, value, 0.0)
        for i, value in enumerate(squares + [jnp.sum(live_rows)])
    )

    grad_out = cotangent[0] * live_rows.astype(bf16)
    down_grads = weight_grads(gated, grad_out)
    down_sum = collect([down_grads[0]], [down_grads[1]], dp_size, True)
    grad_out_later, sends = held(grad_out, next(down_sum))
    down_sends = down_sum.send(sends)
    hidden_later, down_sends = held(hidden, down_sends)
    down_sends = down_sum.send(down_sends)
    grad_hidden = apply_back(grad_out_later, down_pair) * gelu_parts(hidden_later)[1]
    grad_hidden = pick_columns(grad_hidden.astype(bf16), *from_x)
    up_grads = weight_grads(normed_two, grad_hidden)
    up_sum = collect([up_grads[0]], [up_grads[1]], dp_size, True)
    grad_hidden_later, sends = held(grad_hidden, next(up_sum))
    up_sends = up_sum.send(sends)
    grad_normed_two, down_sends = held(apply_back(grad_hidden_later, up_pair), down_sends)
    down_sends = down_sum.send(down_sends)
    grad_mid_norm, grad_norm2_gain, grad_norm2_bias = layer_norm_back(
        grad_normed_two, unit_two, inverse_two, gain_two
    )
    grad_mid_norm, up_sends = held(pick_columns(grad_mid_norm, *from_x), up_sends)
    up_sends = up_sum.send(up_sends)
    grad_middle = grad_out.astype(f32) + grad_mid_norm
    grad_branch = grad_middle.astype(bf16)
    out_grads = weight_grads(attended, grad_branch)
    grad_attended = pick_columns(apply_back(grad_branch, out_pair, bf16), *x_to_groups)
    cut_cols = lambda rows, k: rows[:, k * group : (k + 1) * group]
    grad_heads = jnp.concatenate(
        [cut_cols(grad_attended, 0)]
        + [swap(cut_cols(grad_attended, k), "seq", k, seq_size) for k in range(1, seq_size)],
        axis=0,
    )
    down_cuts = seq_cuts(run(down_sum, down_sends, far - 2)[0], seq_size, seq_at)
    grad_heads, sends = held(grad_heads, tuple(run(up_sum, up_sends, far - 2)) + down_cuts)
    up_sends, down_cuts = sends[:2], sends[2:]
    down_blocks = [down_cuts[0]]
    down_blocks += [swap(down_cuts[k], "seq", k, seq_size) for k in range(1, seq_size)]
    grad_qkv = attend_back(valid_length, query_info, key_info, lse_all, qkv_rows, grad_heads)
    up_cuts = seq_cuts(up_sum.send(up_sends)[0], seq_size, seq_at)
    grad_qkv, sends = held(grad_qkv, up_cuts + tuple(down_blocks))
    up_cuts, down_blocks = sends[:seq_size], sends[seq_size:]
    up_blocks = [up_cuts[0]] + [swap(up_cuts[k], "seq", k, seq_size) for k in range(1, seq_size)]
    part_normed = apply_back(grad_qkv, qkv_pair)
    grad_norm1_gain = jnp.sum(part_normed * unit_all, axis=0)
    grad_norm1_bias = jnp.sum(part_normed, axis=0)
    part_normed = part_normed.astype(bf16)
    column_sums = jnp.sum(grad_qkv.astype(f32), axis=0).reshape(3, 1, group)
    grad_qv_bias = lax.dynamic_update_slice(
        jnp.zeros((2, seq_size, group), f32),
        jnp.concatenate([column_sums[:1], column_sums[2:]], axis=0),
        (0, seq_at, 0),
    )
    grad_out_bias = jnp.sum(grad_branch.astype(f32), axis=0)
    grad_up_bias = jnp.sum(grad_hidden.astype(f32), axis=0)
    grad_down_bias = jnp.sum(grad_out.astype(f32), axis=0)
    by_device = lambda v: v.reshape(dp_size, seq_size, -1)
    plain = [by_device(v) for v in (grad_qv_bias, grad_out_bias, grad_up_bias, grad_down_bias)]
    moved = [by_device(v) for v in (grad_norm1_gain, grad_norm1_bias, grad_norm2_gain, grad_norm2_bias)]
    spare = [jnp.zeros((dp_size, seq_size, 1), f32)] * 2
    plain_x = slotted(spare + plain[:2] + spare + plain[2:])
    plain_x = pick_rows(plain_x.reshape(dp_size, -1), index_of(to_x)).reshape(plain_x.shape)
    spare = spare[:1] * 2
    counts = jnp.broadcast_to(counted, (dp_size, seq_size, 6))
    vec_grads = plain_x + slotted(moved[:2] + spare + moved[2:] + spare + [counts])
    vec_grads = vec_grads.astype(bf16).reshape(2, -1, 128)
    qkv_grads = weight_grads(normed_one, grad_qkv)
    one_sum = collect(
        [qkv_grads[0], vec_grads[0], out_grads[0]],
        [qkv_grads[1], vec_grads[1], out_grads[1]],
        dp_size,
        False,
    )
    odd = next(one_sum)
    part_normed, beside = held(part_normed, (odd[0], odd[2]) + tuple(up_blocks))
    up_blocks = beside[2:]
    sends = run(one_sum, (beside[0], odd[1], beside[1]), far + 1)
    one_cuts = seq_cuts(sends[0], seq_size, seq_at)
    parts = [cut_rows(part_normed, 0)]
    parts += [swap(cut_rows(part_normed, k), "seq", k, seq_size) for k in range(1, seq_size)]
    parts[1], one_cuts = held(parts[1], one_cuts)
    one_blocks = [one_cuts[0]]
    one_blocks += [swap(one_cuts[k], "seq", k, seq_size) for k in range(1, seq_size)]
    grad_normed_one = sum(part.astype(f32) for part in parts)
    unit_one, inverse_one = layer_norm_parts(own_x.astype(f32), gain_one, shift_one)[1:]
    grad_in_norm = layer_norm_back(grad_normed_one, unit_one, inverse_one, gain_one)[0]
    tokens_grad = (grad_middle + pick_columns(grad_in_norm, *from_x)).astype(bf16)[None]
    up_grad = sum(block.astype(f32) for block in up_blocks)
    down_grad = sum(block.astype(f32) for block in down_blocks)
    one_blocks = [block.astype(f32) for block in one_blocks]
    qkv_grad = jnp.stack(
        [part.reshape(rows_one, 3, group) for part in by_place([b[:, : 3 * group] for b in one_blocks], seq_at)],
        axis=2,
    ).reshape(rows_one, 3 * width)
    rest_sum = sum(block[:, 3 * group :] for block in one_blocks)
    vec_sum, out_grad = rest_sum[:, :128], rest_sum[:, 128:]
    n1g, n1b, qvb, ob, n2g, n2b, ub, db, counted = [from_slot(vec_sum, i) for i in range(slots)]
    residual_rms = jnp.sqrt(counted[:5] / (counted[5] * width))

    return (
        output,
        tokens_grad,
        n1g,
        n1b,
        qkv_grad,
        qvb,
        out_grad,
        ob,
        n2g,
        n2b,
        up_grad,
        ub,
        down_grad,
        db,
        residual_rms,
    )


def solution(mesh):
    return jax.shard_map(
        per_device,
        mesh=mesh,
        in_specs=(
            P("dp", "seq", None),
            P("dp", "seq", None),
            P("dp"),
            P("dp", None),
            P("dp", None),
            P(("dp", "seq")),
            P(("dp", "seq")),
            P(("dp", "seq"), None),
            P(("dp", "seq")),
            P(("dp", "seq"), None),
            P(("dp", "seq")),
            P(("dp", "seq")),
            P(("dp", "seq")),
            P(("dp", "seq"), None),
            P(("dp", "seq")),
            P(("dp", "seq"), None),
            P(("dp", "seq")),
        ),
        out_specs=(
            P("dp", "seq", None),
            P("dp", "seq", None),
            P(("dp", "seq")),
            P(("dp", "seq")),
            P(("dp", "seq"), None),
            P(("dp", "seq")),
            P(("dp", "seq"), None),
            P(("dp", "seq")),
            P(("dp", "seq")),
            P(("dp", "seq")),
            P(("dp", "seq"), None),
            P(("dp", "seq")),
            P(("dp", "seq"), None),
            P(("dp", "seq")),
            P(),
        ),
        check_vma=False,
    )
```

```python
import functools

import jax
import jax.numpy as jnp
from jax import lax
from jax.experimental import pallas as pl
from jax.experimental.pallas import tpu as pltpu
from jax.sharding import PartitionSpec as P

HEAD_DIM = 64
PIECE = 256


gelu_scale = 0.7978845608028654
gelu_cubic = 0.044715


def layer_norm_parts(rows_in, gain, shift):
    mean_row = jnp.mean(rows_in, axis=-1, keepdims=True)
    centered = rows_in - mean_row
    inverse = lax.rsqrt(jnp.mean(centered * centered, axis=-1, keepdims=True) + 1e-05)
    unit_rows = centered * inverse
    return (unit_rows * gain + shift, unit_rows, inverse)


def layer_norm_back(grad_in, unit_rows, inverse, gain):
    scaled = grad_in * gain
    back_rows = inverse * (
        scaled
        - jnp.mean(scaled, axis=-1, keepdims=True)
        - unit_rows * jnp.mean(scaled * unit_rows, axis=-1, keepdims=True)
    )
    return (back_rows, jnp.sum(grad_in * unit_rows, axis=0), jnp.sum(grad_in, axis=0))


def gelu_parts(values):
    tangent = jnp.tanh(gelu_scale * (values + gelu_cubic * values * values * values))
    slope = 0.5 * (1.0 + tangent) + 0.5 * values * (1.0 - tangent * tangent) * gelu_scale * (
        1.0 + 3.0 * gelu_cubic * values * values
    )
    return (0.5 * values * (1.0 + tangent), slope)


def piece_labels(positions, starts):
    inside = (positions[:, :, None] >= starts[:, None, :]) & (
        positions[:, :, None] < starts[:, None, :] + PIECE
    )
    labels = jnp.arange(1, starts.shape[1] + 1, dtype=jnp.int32)
    return jnp.sum(jnp.where(inside, labels[None, None, :], 0), axis=2)


def swap(value, axis, bit, size):
    return lax.ppermute(value, axis, [(i, i ^ bit) for i in range(size)])


def doubled(bits):
    order = [0]
    for bit in bits:
        order = order + [at ^ bit for at in order]
    return order


def far_bits(dp_size):
    bits = [1 << i for i in range(1, dp_size.bit_length() - 1)]
    half = (len(bits) + 1) // 2
    return bits, bits[half:] + bits[:half]


def add(left, right):
    return (left.astype(jnp.float32) + right.astype(jnp.float32)).astype(left.dtype)


def by_place(blocks, me):
    out, bit = list(blocks), 1
    while bit < len(out):
        odd = jnp.bitwise_and(me, bit) > 0
        out = [jnp.where(odd, out[i ^ bit], out[i]) for i in range(len(out))]
        bit *= 2
    return out


def pick_columns_body(table, flip_ref, in_ref, out_ref):
    width = out_ref.shape[1] // len(table)
    for i, entry in enumerate(table):
        at = pl.multiple_of(jnp.bitwise_xor(flip_ref[0], entry) * width, width)
        out_ref[:, i * width : (i + 1) * width] = in_ref[:, pl.ds(at, width)]


def pick_columns(rows, table, flip):
    width = rows.shape[1] // len(table)
    if width % 128:
        parts = [
            lax.dynamic_slice_in_dim(rows, jnp.bitwise_xor(flip, entry) * width, width, 1)
            for entry in table
        ]
        return jnp.concatenate(parts, axis=1)
    return pl.pallas_call(
        functools.partial(pick_columns_body, table),
        out_shape=jax.ShapeDtypeStruct(rows.shape, rows.dtype),
        in_specs=[
            pl.BlockSpec(memory_space=pltpu.SMEM),
            pl.BlockSpec(memory_space=pltpu.VMEM),
        ],
        out_specs=pl.BlockSpec(memory_space=pltpu.VMEM),
        name="pick_columns",
    )(flip.reshape(1), rows)


def pick_rows(table, index):
    chosen = index[:, None] == jnp.arange(table.shape[0], dtype=jnp.int32)[None, :]
    return jnp.sum(jnp.where(chosen[:, :, None], table[None], 0.0), axis=1)


def held(value, beside):
    out = lax.optimization_barrier((value,) + tuple(beside))
    return out[0], out[1:]


def place_rows_body(plan, *refs):
    ins, out, held_ref, sems = refs[:-3], refs[-3], refs[-2], refs[-1]
    copies_in, copies_out = [], []
    for i, (source, low, rows, high) in enumerate(plan):
        middle = held_ref.at[high : high + rows, :]
        copies_in.append(
            pltpu.make_async_copy(ins[source].at[low : low + rows, :], middle, sems.at[0, i])
        )
        copies_out.append(
            pltpu.make_async_copy(middle, out.at[high : high + rows, :], sems.at[1, i])
        )
    for copy in copies_in:
        copy.start()
    for copy_in, copy_out in zip(copies_in, copies_out):
        copy_in.wait()
        copy_out.start()
    for copy in copies_out:
        copy.wait()


def place_rows(parts, plan):
    rows, cols = sum(entry[2] for entry in plan), parts[0].shape[1]
    size = rows * cols * parts[0].dtype.itemsize
    return pl.pallas_call(
        functools.partial(place_rows_body, plan),
        out_shape=jax.ShapeDtypeStruct((rows, cols), parts[0].dtype),
        in_specs=[pl.BlockSpec(memory_space=pl.ANY)] * len(parts),
        out_specs=pl.BlockSpec(memory_space=pl.ANY),
        scratch_shapes=[
            pltpu.VMEM((rows, cols), parts[0].dtype),
            pltpu.SemaphoreType.DMA((2, len(plan))),
        ],
        cost_estimate=pl.CostEstimate(flops=0, transcendentals=0, bytes_accessed=2 * size),
        name="place_rows",
    )(*parts)


def spread(piece, dp_size, split):
    rows = piece.shape[0]
    bits_x, bits_y = far_bits(dp_size)
    order = doubled(bits_x)
    parts, plans = (piece,), (bits_x,)
    if split:
        parts, plans = (piece[: rows // 2], piece[rows // 2 :]), (bits_x, bits_y)
    for step in range(len(bits_x)):
        parts = yield tuple(parts)
        got = [swap(part, "dp", bits[step], dp_size) for part, bits in zip(parts, plans)]
        if step + 1 < len(bits_x):
            parts = [jnp.concatenate(pair, axis=0) for pair in zip(parts, got)]
    got = yield tuple(got)
    if split:
        half, order_y, plan = rows // 2, doubled(bits_y), []
        count = len(order) // 2
        for i, at in enumerate(order):
            for side, places in enumerate((order, order_y)):
                j = places.index(at)
                source = side if j < count else 2 + side
                plan.append((source, (j % count) * half, half, (2 * i + side) * half))
        own = place_rows(list(parts) + list(got), plan)
    else:
        own = jnp.concatenate([parts[0], got[0]], axis=0)
    (own,) = yield (own,)
    yield own, swap(own, "dp", 1, dp_size)


def run(stages, values, count):
    for _ in range(count):
        values = stages.send(values)
    return values


def collect(own, odd, dp_size, split):
    bits_x, bits_y = far_bits(dp_size)
    order, count = doubled(bits_x), dp_size // 2
    odd = yield tuple(odd)
    got = [swap(part, "dp", 1, dp_size) for part in odd]
    stacks = [
        (a.reshape(count, -1, a.shape[1]), b.reshape(count, -1, a.shape[1]))
        for a, b in zip(own, got)
    ]
    rows = stacks[0][0].shape[1]

    def taken(which, low, high):
        cols = [
            jnp.concatenate([add(a[i, low:high], b[i, low:high]) for a, b in stacks], axis=1)
            for i in which
        ]
        return jnp.stack(cols)

    plans = [(bits_x, 0, rows)]
    if split:
        plans = [(bits_x, 0, rows // 2), (bits_y, rows // 2, rows)]
    keeps, sends = [], []
    half = count // 2
    for bits, low, high in plans:
        places = [order.index(at) for at in doubled(bits)]
        keeps.append(taken(places[:half], low, high))
        sends.append(taken(places[half:], low, high))
    for step in reversed(range(len(bits_x))):
        sends = yield tuple(sends)
        got = [swap(send, "dp", bits[step], dp_size) for send, (bits, _, _) in zip(sends, plans)]
        if step:
            cut = (1 << step) // 2
            sends = [add(keep[cut:], new[cut:]) for keep, new in zip(keeps, got)]
            keeps = [add(keep[:cut], new[:cut]) for keep, new in zip(keeps, got)]
        else:
            keeps = [add(keep, new)[0] for keep, new in zip(keeps, got)]
    yield (jnp.concatenate(keeps, axis=0),)


def seq_gather(shard, seq_size, earlier=None):
    out, earlier = [shard], list(earlier) if earlier else None
    for k in range(1, seq_size):
        sent = shard
        if earlier:
            sent, (earlier[k],) = held(shard, (earlier[k],))
        out.append(swap(sent, "seq", k, seq_size))
    return out, earlier


def seq_cuts(piece, seq_size, seq_at):
    rows = piece.shape[0] // seq_size
    return tuple(
        lax.dynamic_slice_in_dim(piece, jnp.bitwise_xor(seq_at, k) * rows, rows, 0)
        for k in range(seq_size)
    )


def dot(left, right):
    return jnp.dot(left, right, preferred_element_type=jnp.float32)


def dot_back(grad, weight):
    return jnp.einsum("rn,kn->rk", grad, weight, preferred_element_type=jnp.float32)


def dot_rows(rows, grad):
    return jnp.einsum("rk,rn->kn", rows, grad, preferred_element_type=jnp.float32)


def apply(rows, pair):
    half = rows.shape[1] // 2
    return dot(rows[:, :half], pair[0]) + dot(rows[:, half:], pair[1])


def apply_back(grad, pair, dtype=jnp.float32):
    return jnp.concatenate([dot_back(grad, part).astype(dtype) for part in pair], axis=1)


def weight_grads(rows, grad):
    half = rows.shape[1] // 2
    return [dot_rows(part, grad).astype(jnp.bfloat16) for part in (rows[:, :half], rows[:, half:])]


def seen(valid_ref, query_ref, key_ref):
    valid = valid_ref[0]
    query_at, query_seg, query_piece = (query_ref[:, i : i + 1] for i in range(3))
    key_at, key_seg, key_piece = (key_ref[i : i + 1, :] for i in range(3))
    together = (query_piece == key_piece) & (query_piece > 0)
    rule_ok = (query_seg == key_seg) & ((key_at <= query_at) | together)
    allowed = (key_at < valid) & ((query_at >= valid) | rule_ok)
    return jnp.where(allowed, 0.0, -1e30)


def one_head(rows, head):
    lane = lax.broadcasted_iota(jnp.int32, rows.shape, 1)
    return jnp.where(lane // HEAD_DIM == head, rows, jnp.zeros_like(rows))


def contract(left, right, dims):
    return lax.dot_general(left, right, (dims, ((), ())), preferred_element_type=jnp.float32)


def attend_body(valid_ref, query_ref, key_ref, q_ref, k_ref, v_ref, out_ref, lse_ref):
    hidden_keys = seen(valid_ref, query_ref, key_ref)
    columns = []
    for at in range(0, q_ref.shape[1], 128):
        pair = slice(at, at + 128)
        query, key, value = q_ref[:, pair], k_ref[:, pair], v_ref[:, pair]
        outs = []
        for head in range(128 // HEAD_DIM):
            raw = contract(one_head(query, head), key, ((1,), (1,)))
            raw = raw * HEAD_DIM ** (-0.5) + hidden_keys
            top = jnp.max(raw, axis=-1, keepdims=True)
            expo = jnp.exp(raw - top)
            total = jnp.sum(expo, axis=-1, keepdims=True)
            probs = (expo * (1.0 / total)).astype(jnp.bfloat16)
            outs.append(contract(probs, value, ((1,), (0,))))
            columns.append(top + jnp.log(total))
        lane = lax.broadcasted_iota(jnp.int32, outs[0].shape, 1)
        out_ref[:, pair] = jnp.where(lane < HEAD_DIM, outs[0], outs[1]).astype(out_ref.dtype)
    for i, column in enumerate(columns):
        lse_ref[:, i : i + 1] = column


def attend_back_body(
    valid_ref, query_ref, key_ref, lse_ref, q_ref, k_ref, v_ref, grad_ref, out_ref, sum_ref
):
    step, group = pl.program_id(0), q_ref.shape[1]
    rows = q_ref.shape[0]

    @pl.when(step == 0)
    def _():
        sum_ref[...] = jnp.zeros_like(sum_ref)

    hidden_keys = seen(valid_ref, query_ref, key_ref)
    at_rows = pl.ds(pl.multiple_of(step * rows, rows), rows)
    scale = HEAD_DIM ** (-0.5)
    for at in range(0, group, 128):
        pair = slice(at, at + 128)
        query, key, value, grad = q_ref[:, pair], k_ref[:, pair], v_ref[:, pair], grad_ref[:, pair]
        grad_query = grad_key = grad_value = 0.0
        for head in range(128 // HEAD_DIM):
            column = at // HEAD_DIM + head
            own_query, own_grad = one_head(query, head), one_head(grad, head)
            raw = contract(own_query, key, ((1,), (1,))) * scale + hidden_keys
            probs = jnp.exp(raw - lse_ref[:, column : column + 1])
            grad_probs = contract(own_grad, value, ((1,), (1,)))
            inner = jnp.sum(probs * grad_probs, axis=-1, keepdims=True)
            grad_scores = (probs * (grad_probs - inner)).astype(jnp.bfloat16)
            grad_value += contract(probs.astype(jnp.bfloat16), own_grad, ((0,), (0,)))
            grad_key += contract(grad_scores, own_query, ((0,), (0,)))
            grad_query += contract(grad_scores, one_head(key, head), ((1,), (0,)))
        out_ref[at_rows, pair] = (grad_query * scale).astype(out_ref.dtype)
        sum_ref[:, pair] += grad_key
        sum_ref[:, group + at : group + at + 128] += grad_value

    @pl.when(step == pl.num_programs(0) - 1)
    def _():
        out_ref[:, group : 2 * group] = (sum_ref[:, :group] * scale).astype(out_ref.dtype)
        out_ref[:, 2 * group :] = sum_ref[:, group:].astype(out_ref.dtype)


def attention_specs(length, group, block):
    whole = lambda column: pl.BlockSpec((length, group), lambda i: (0, column))
    return [
        pl.BlockSpec(memory_space=pltpu.SMEM),
        pl.BlockSpec((block, 3), lambda i: (i, 0)),
        pl.BlockSpec((3, length), lambda i: (0, 0)),
    ], [pl.BlockSpec((block, group), lambda i: (i, 0)), whole(1), whole(2)]


def attend(valid, query_info, key_info, qkv_rows, block=256):
    length, group = qkv_rows.shape[0], qkv_rows.shape[1] // 3
    heads = group // HEAD_DIM
    info_specs, qkv_specs = attention_specs(length, group, block)
    work = heads * length * length
    return pl.pallas_call(
        attend_body,
        grid=(length // block,),
        in_specs=info_specs + qkv_specs,
        out_specs=[
            pl.BlockSpec((block, group), lambda i: (i, 0)),
            pl.BlockSpec((block, heads), lambda i: (i, 0)),
        ],
        out_shape=[
            jax.ShapeDtypeStruct((length, group), jnp.bfloat16),
            jax.ShapeDtypeStruct((length, heads), jnp.float32),
        ],
        cost_estimate=pl.CostEstimate(
            flops=16 * work * HEAD_DIM, transcendentals=work, bytes_accessed=32 * length * group
        ),
        name="attend",
    )(valid, query_info, key_info, qkv_rows, qkv_rows, qkv_rows)


def attend_back(valid, query_info, key_info, lse, qkv_rows, grad_rows, block=256):
    length, group = grad_rows.shape
    heads = group // HEAD_DIM
    info_specs, qkv_specs = attention_specs(length, group, block)
    work = heads * length * length
    return pl.pallas_call(
        attend_back_body,
        grid=(length // block,),
        in_specs=info_specs
        + [pl.BlockSpec((block, heads), lambda i: (i, 0))]
        + qkv_specs
        + [pl.BlockSpec((block, group), lambda i: (i, 0))],
        out_specs=pl.BlockSpec((length, 3 * group), lambda i: (0, 0)),
        out_shape=jax.ShapeDtypeStruct((length, 3 * group), jnp.bfloat16),
        scratch_shapes=[pltpu.VMEM((length, 2 * group), jnp.float32)],
        cost_estimate=pl.CostEstimate(
            flops=40 * work * HEAD_DIM, transcendentals=work, bytes_accessed=64 * length * group
        ),
        name="attend_back",
    )(valid, query_info, key_info, lse, qkv_rows, qkv_rows, qkv_rows, grad_rows)


def per_device(
    tokens,
    cotangent,
    valid_length,
    segment_ids,
    piece_starts,
    norm1_gain,
    norm1_bias,
    qkv_weight,
    qv_bias,
    out_weight,
    out_bias,
    norm2_gain,
    norm2_bias,
    up_weight,
    up_bias,
    down_weight,
    down_bias,
):
    f32, bf16 = jnp.float32, jnp.bfloat16
    _, local_len, width = tokens.shape
    dp_size, seq_size = lax.axis_size("dp"), lax.axis_size("seq")
    dp_at, seq_at = lax.axis_index("dp"), lax.axis_index("seq")
    devices = dp_size * seq_size
    group = width // seq_size

    half_order = doubled(far_bits(dp_size)[0])
    full = half_order + [at ^ 1 for at in half_order]
    back = [full.index(at) for at in range(dp_size)]
    place_in_x = lambda block: sum(
        jnp.where(jnp.bitwise_and(block, 1 << i) > 0, back[1 << i], 0)
        for i in range(dp_size.bit_length() - 1)
    )
    to_x, from_x = (full, dp_at), (back, place_in_x(dp_at))
    in_groups = jnp.bitwise_xor(dp_at, seq_at * (dp_size // seq_size))
    groups_to_x, x_to_groups = (full, in_groups), (back, place_in_x(in_groups))
    index_of = lambda rule: jnp.bitwise_xor(jnp.array(rule[0], jnp.int32), rule[1])

    vectors = (norm1_gain, norm1_bias, qv_bias, out_bias, norm2_gain, norm2_bias, up_bias, down_bias)
    widths = [v.shape[0] for v in vectors]
    rows_one = qkv_weight.shape[0]
    slots = len(vectors) + 1
    in_row = -(-slots // rows_one)
    slot = 128 // in_row
    vec_rows = -(-slots // in_row)

    def slotted(parts):
        rows = []
        for at in range(0, len(parts), in_row):
            row = [
                jnp.pad(v, [(0, 0)] * (v.ndim - 1) + [(0, slot - v.shape[-1])])
                for v in parts[at : at + in_row]
            ]
            row = jnp.concatenate(row, axis=-1) if in_row > 1 else row[0]
            rows.append(jnp.pad(row, [(0, 0)] * (row.ndim - 1) + [(0, 128 - row.shape[-1])]))
        return jnp.stack(rows, axis=-2)

    def whole_rows(rows):
        return jnp.pad(rows, [(0, 0)] * (rows.ndim - 2) + [(0, rows_one - rows.shape[-2]), (0, 0)])

    def from_slot(table, which):
        row, low = which // in_row, (which % in_row) * slot
        size = widths[which] if which < len(widths) else 6
        return table[..., row, low : low + size]

    vec_block = whole_rows(slotted(vectors))
    qkv_split = qkv_weight.reshape(rows_one, 3, seq_size, group)

    def qkv_part(k):
        mine = lax.dynamic_index_in_dim(qkv_split, jnp.bitwise_xor(seq_at, k), 2, keepdims=False)
        return jnp.concatenate([mine.reshape(rows_one, 3 * group), vec_block], axis=1)

    first = [qkv_part(0)] + [swap(qkv_part(k), "seq", k, seq_size) for k in range(1, seq_size)]
    own_x = pick_columns(tokens[0], *to_x)
    second, _ = seq_gather(jnp.concatenate([out_weight, up_weight], axis=1), seq_size)
    token_blocks = [own_x]
    for k in range(1, seq_size):
        sent, (first[k], second[k]) = held(own_x, (first[k], second[k]))
        token_blocks.append(swap(sent, "seq", k, seq_size))
    far = dp_size.bit_length() - 2
    stacked = lambda blocks: jnp.concatenate(by_place(blocks, seq_at), axis=0)
    one_parts = spread(stacked(first), dp_size, False)
    one_pair = run(one_parts, next(one_parts), far + 2)
    two_parts = spread(stacked(second), dp_size, True)
    two_sends = run(two_parts, next(two_parts), far - 1)
    token_blocks[0], beside = held(token_blocks[0], tuple(token_blocks[1:]) + two_sends)
    token_blocks = token_blocks[:1] + list(beside[: seq_size - 1])
    got = two_parts.send(beside[seq_size - 1 :])
    third, token_blocks = seq_gather(down_weight, seq_size, token_blocks)
    qkv_pair = [part[:, : 3 * group] for part in one_pair]

    vec_x = jnp.concatenate([part[:, 3 * group :] for part in one_pair], axis=0).astype(f32)
    vec_x = vec_x.reshape(dp_size, seq_size, rows_one, 128)[:, :, :vec_rows]
    vec_n = pick_rows(vec_x.reshape(dp_size, -1), index_of(from_x)).reshape(vec_x.shape)

    field = lambda table, which: from_slot(table, which).reshape(-1)
    gain_one, shift_one, gain_two, shift_two = [field(vec_x, i) for i in (0, 1, 4, 5)]
    qv_full, out_shift, up_shift, down_shift = [field(vec_n, i) for i in (2, 3, 6, 7)]

    starts = [jnp.bitwise_xor(seq_at, k) * local_len for k in range(seq_size)]
    step = jnp.arange(local_len, dtype=jnp.int32)
    place = jnp.concatenate([at + step for at in starts])
    segments = jnp.concatenate(
        [lax.dynamic_slice_in_dim(segment_ids, at, local_len, 1) for at in starts], axis=1
    )
    pieces = piece_labels(place[None, :], piece_starts)
    key_info = jnp.concatenate([place[None], segments, pieces], axis=0)
    query_info = key_info.T
    live_rows = (starts[0] + step < valid_length[0]).astype(f32)[:, None]

    all_x = jnp.concatenate(token_blocks, axis=0).astype(f32)
    normed_one, unit_all, _ = layer_norm_parts(all_x, gain_one, shift_one)
    normed_one = normed_one.astype(bf16)
    half_bias = qv_full.reshape(2, seq_size, group)
    half_bias = lax.dynamic_index_in_dim(half_bias, seq_at, 1, keepdims=False)
    qkv_shift = jnp.concatenate([half_bias[0], jnp.zeros((group,), f32), half_bias[1]])
    qkv_rows = (apply(normed_one, qkv_pair) + qkv_shift).astype(bf16)
    attended_rows, lse_all = attend(valid_length, query_info, key_info, qkv_rows)
    attended_rows, beside = held(attended_rows, tuple(third) + tuple(got))
    third, got = beside[:-2], beside[-2:]
    cut_rows = lambda rows, k: rows[k * local_len : (k + 1) * local_len]
    attended = [cut_rows(attended_rows, 0)] + [
        swap(cut_rows(attended_rows, k), "seq", k, seq_size) for k in range(1, seq_size)
    ]
    own, (piece,) = held(two_parts.send(got)[0], (stacked(third),))
    two_pair = two_parts.send((own,))
    out_pair = [part[:, :width] for part in two_pair]
    up_pair = [part[:, width:] for part in two_pair]
    down_parts = spread(piece, dp_size, True)
    down_sends = run(down_parts, next(down_parts), far - 1)

    attended, down_sends = held(jnp.concatenate(attended, axis=1), down_sends)
    got = down_parts.send(down_sends)
    attended = pick_columns(attended, *groups_to_x)
    branch = apply(attended, out_pair) + out_shift
    tokens_f = tokens[0].astype(f32)
    middle = tokens_f + branch
    middle_x = pick_columns(middle, *to_x)
    normed_two, unit_two, inverse_two = layer_norm_parts(middle_x, gain_two, shift_two)
    normed_two = normed_two.astype(bf16)
    hidden = pick_columns(apply(normed_two, up_pair) + up_shift, *to_x)
    hidden, got = held(hidden, got)
    down_pair = run(down_parts, got, 2)
    gated = gelu_parts(hidden)[0].astype(bf16)
    grad_out = cotangent[0] * live_rows.astype(bf16)
    down_grads = weight_grads(gated, grad_out)
    down_sum = collect([down_grads[0]], [down_grads[1]], dp_size, True)
    grad_out_later, sends = held(grad_out, next(down_sum))
    down_sends = down_sum.send(sends)
    hidden_later, down_sends = held(hidden, down_sends)
    down_sends = down_sum.send(down_sends)
    grad_hidden = apply_back(grad_out_later, down_pair) * gelu_parts(hidden_later)[1]
    grad_hidden = pick_columns(grad_hidden.astype(bf16), *from_x)
    up_grads = weight_grads(normed_two, grad_hidden)
    up_sum = collect([up_grads[0]], [up_grads[1]], dp_size, True)
    grad_hidden_later, sends = held(grad_hidden, next(up_sum))
    up_sends = up_sum.send(sends)
    grad_normed_two = apply_back(grad_hidden_later, up_pair)
    grad_mid_norm, grad_norm2_gain, grad_norm2_bias = layer_norm_back(
        grad_normed_two, unit_two, inverse_two, gain_two
    )
    grad_mid_norm = pick_columns(grad_mid_norm, *from_x)
    grad_middle = grad_out.astype(f32) + grad_mid_norm
    grad_branch = grad_middle.astype(bf16)
    out_grads = weight_grads(attended, grad_branch)
    grad_attended = pick_columns(apply_back(grad_branch, out_pair, bf16), *x_to_groups)
    grad_attended, (gated_later,) = held(grad_attended, (gated,))
    mlp_out = apply(gated_later, down_pair) + down_shift
    result = middle + mlp_out
    output = result.astype(bf16)[None]
    squares = [
        jnp.sum(live_rows * entry * entry)
        for entry in (tokens_f, branch, middle, mlp_out, result)
    ]
    slots_at = jnp.arange(6, dtype=jnp.int32)
    counted = sum(
        jnp.where(slots_at == i, value, 0.0)
        for i, value in enumerate(squares + [jnp.sum(live_rows)])
    )
    cut_cols = lambda rows, k: rows[:, k * group : (k + 1) * group]
    grad_heads = jnp.concatenate(
        [cut_cols(grad_attended, 0)]
        + [swap(cut_cols(grad_attended, k), "seq", k, seq_size) for k in range(1, seq_size)],
        axis=0,
    )
    grad_heads, sends = held(grad_heads, tuple(down_sends) + tuple(up_sends))
    down_cuts = seq_cuts(run(down_sum, sends[:2], far - 1)[0], seq_size, seq_at)
    up_sends = run(up_sum, sends[2:], far - 1)
    grad_qkv = attend_back(valid_length, query_info, key_info, lse_all, qkv_rows, grad_heads)
    grad_qkv, down_cuts = held(grad_qkv, down_cuts)
    down_blocks = [down_cuts[0]]
    down_blocks += [swap(down_cuts[k], "seq", k, seq_size) for k in range(1, seq_size)]
    part_normed = apply_back(grad_qkv, qkv_pair)
    grad_norm1_gain = jnp.sum(part_normed * unit_all, axis=0)
    grad_norm1_bias = jnp.sum(part_normed, axis=0)
    part_normed = part_normed.astype(bf16)
    column_sums = jnp.sum(grad_qkv.astype(f32), axis=0).reshape(3, 1, group)
    grad_qv_bias = lax.dynamic_update_slice(
        jnp.zeros((2, seq_size, group), f32),
        jnp.concatenate([column_sums[:1], column_sums[2:]], axis=0),
        (0, seq_at, 0),
    )
    grad_out_bias = jnp.sum(grad_branch.astype(f32), axis=0)
    grad_up_bias = jnp.sum(grad_hidden.astype(f32), axis=0)
    grad_down_bias = jnp.sum(grad_out.astype(f32), axis=0)
    by_device = lambda v: v.reshape(dp_size, seq_size, -1)
    plain = [by_device(v) for v in (grad_qv_bias, grad_out_bias, grad_up_bias, grad_down_bias)]
    moved = [by_device(v) for v in (grad_norm1_gain, grad_norm1_bias, grad_norm2_gain, grad_norm2_bias)]
    spare = [jnp.zeros((dp_size, seq_size, 1), f32)] * 2
    counts = jnp.broadcast_to(counted, (dp_size, seq_size, 6))
    plain_x = slotted(spare + plain[:2] + spare + plain[2:] + [counts])
    plain_x = pick_rows(plain_x.reshape(dp_size, -1), index_of(to_x)).reshape(plain_x.shape)
    spare = spare[:1] * 2
    vec_grads = plain_x + slotted(moved[:2] + spare + moved[2:] + spare + spare[:1])
    vec_grads = whole_rows(vec_grads.astype(bf16)).reshape(2, -1, 128)
    qkv_grads = weight_grads(normed_one, grad_qkv)
    one_sum = collect(
        [qkv_grads[0], vec_grads[0], out_grads[0]],
        [qkv_grads[1], vec_grads[1], out_grads[1]],
        dp_size,
        False,
    )
    odd = next(one_sum)
    part_normed, beside = held(
        part_normed, (odd[0], odd[2]) + tuple(up_sends) + tuple(down_blocks)
    )
    up_cuts = seq_cuts(up_sum.send(beside[2:4])[0], seq_size, seq_at)
    down_blocks = beside[4:]
    sends = run(one_sum, (beside[0], odd[1], beside[1]), far + 1)
    one_cuts = seq_cuts(sends[0], seq_size, seq_at)
    parts = [cut_rows(part_normed, 0)]
    parts += [swap(cut_rows(part_normed, k), "seq", k, seq_size) for k in range(1, seq_size)]
    parts[1], beside = held(parts[1], one_cuts + up_cuts)
    one_cuts, up_cuts = beside[:seq_size], beside[seq_size:]
    up_blocks = [up_cuts[0]] + [swap(up_cuts[k], "seq", k, seq_size) for k in range(1, seq_size)]
    one_blocks = [one_cuts[0]]
    one_blocks += [swap(one_cuts[k], "seq", k, seq_size) for k in range(1, seq_size)]
    grad_normed_one = sum(part.astype(f32) for part in parts)
    unit_one, inverse_one = layer_norm_parts(own_x.astype(f32), gain_one, shift_one)[1:]
    grad_in_norm = layer_norm_back(grad_normed_one, unit_one, inverse_one, gain_one)[0]
    tokens_grad = (grad_middle + pick_columns(grad_in_norm, *from_x)).astype(bf16)[None]
    tokens_grad, up_blocks = held(tokens_grad, up_blocks)
    up_grad = sum(block.astype(f32) for block in up_blocks)
    down_grad = sum(block.astype(f32) for block in down_blocks)
    one_blocks = [block.astype(f32) for block in one_blocks]
    qkv_grad = jnp.stack(
        [part.reshape(rows_one, 3, group) for part in by_place([b[:, : 3 * group] for b in one_blocks], seq_at)],
        axis=2,
    ).reshape(rows_one, 3 * width)
    rest_sum = sum(block[:, 3 * group :] for block in one_blocks)
    vec_sum, out_grad = rest_sum[:, :128], rest_sum[:, 128:]
    n1g, n1b, qvb, ob, n2g, n2b, ub, db, counted = [from_slot(vec_sum, i) for i in range(slots)]
    residual_rms = jnp.sqrt(counted[:5] / (counted[5] * width))

    return (
        output,
        tokens_grad,
        n1g,
        n1b,
        qkv_grad,
        qvb,
        out_grad,
        ob,
        n2g,
        n2b,
        up_grad,
        ub,
        down_grad,
        db,
        residual_rms,
    )


def solution(mesh):
    return jax.shard_map(
        per_device,
        mesh=mesh,
        in_specs=(
            P("dp", "seq", None),
            P("dp", "seq", None),
            P("dp"),
            P("dp", None),
            P("dp", None),
            P(("dp", "seq")),
            P(("dp", "seq")),
            P(("dp", "seq"), None),
            P(("dp", "seq")),
            P(("dp", "seq"), None),
            P(("dp", "seq")),
            P(("dp", "seq")),
            P(("dp", "seq")),
            P(("dp", "seq"), None),
            P(("dp", "seq")),
            P(("dp", "seq"), None),
            P(("dp", "seq")),
        ),
        out_specs=(
            P("dp", "seq", None),
            P("dp", "seq", None),
            P(("dp", "seq")),
            P(("dp", "seq")),
            P(("dp", "seq"), None),
            P(("dp", "seq")),
            P(("dp", "seq"), None),
            P(("dp", "seq")),
            P(("dp", "seq")),
            P(("dp", "seq")),
            P(("dp", "seq"), None),
            P(("dp", "seq")),
            P(("dp", "seq"), None),
            P(("dp", "seq")),
            P(),
        ),
        check_vma=False,
    )
```

```python
import functools

import jax
import jax.numpy as jnp
from jax import lax
from jax.experimental import pallas as pl
from jax.experimental.pallas import tpu as pltpu
from jax.sharding import PartitionSpec as P

HEAD_DIM = 64
PIECE = 256


gelu_scale = 0.7978845608028654
gelu_cubic = 0.044715


def layer_norm_parts(rows_in, gain, shift):
    mean_row = jnp.mean(rows_in, axis=-1, keepdims=True)
    centered = rows_in - mean_row
    inverse = lax.rsqrt(jnp.mean(centered * centered, axis=-1, keepdims=True) + 1e-05)
    unit_rows = centered * inverse
    return (unit_rows * gain + shift, unit_rows, inverse)


def layer_norm_back(grad_in, unit_rows, inverse, gain):
    scaled = grad_in * gain
    back_rows = inverse * (
        scaled
        - jnp.mean(scaled, axis=-1, keepdims=True)
        - unit_rows * jnp.mean(scaled * unit_rows, axis=-1, keepdims=True)
    )
    return (back_rows, jnp.sum(grad_in * unit_rows, axis=0), jnp.sum(grad_in, axis=0))


def gelu_parts(values):
    tangent = jnp.tanh(gelu_scale * (values + gelu_cubic * values * values * values))
    slope = 0.5 * (1.0 + tangent) + 0.5 * values * (1.0 - tangent * tangent) * gelu_scale * (
        1.0 + 3.0 * gelu_cubic * values * values
    )
    return (0.5 * values * (1.0 + tangent), slope)


def piece_labels(positions, starts):
    inside = (positions[:, :, None] >= starts[:, None, :]) & (
        positions[:, :, None] < starts[:, None, :] + PIECE
    )
    labels = jnp.arange(1, starts.shape[1] + 1, dtype=jnp.int32)
    return jnp.sum(jnp.where(inside, labels[None, None, :], 0), axis=2)


def swap(value, axis, bit, size):
    return lax.ppermute(value, axis, [(i, i ^ bit) for i in range(size)])


def doubled(bits):
    order = [0]
    for bit in bits:
        order = order + [at ^ bit for at in order]
    return order


def far_bits(dp_size):
    bits = [1 << i for i in range(1, dp_size.bit_length() - 1)]
    half = (len(bits) + 1) // 2
    return bits, bits[half:] + bits[:half]


def add(left, right):
    return (left.astype(jnp.float32) + right.astype(jnp.float32)).astype(left.dtype)


def by_place(blocks, me):
    out, bit = list(blocks), 1
    while bit < len(out):
        odd = jnp.bitwise_and(me, bit) > 0
        out = [jnp.where(odd, out[i ^ bit], out[i]) for i in range(len(out))]
        bit *= 2
    return out


def pick_columns_body(table, flip_ref, in_ref, out_ref):
    width = out_ref.shape[1] // len(table)
    for i, entry in enumerate(table):
        at = pl.multiple_of(jnp.bitwise_xor(flip_ref[0], entry) * width, width)
        out_ref[:, i * width : (i + 1) * width] = in_ref[:, pl.ds(at, width)]


def pick_columns(rows, table, flip):
    width = rows.shape[1] // len(table)
    if width % 128:
        parts = [
            lax.dynamic_slice_in_dim(rows, jnp.bitwise_xor(flip, entry) * width, width, 1)
            for entry in table
        ]
        return jnp.concatenate(parts, axis=1)
    return pl.pallas_call(
        functools.partial(pick_columns_body, table),
        out_shape=jax.ShapeDtypeStruct(rows.shape, rows.dtype),
        in_specs=[
            pl.BlockSpec(memory_space=pltpu.SMEM),
            pl.BlockSpec(memory_space=pltpu.VMEM),
        ],
        out_specs=pl.BlockSpec(memory_space=pltpu.VMEM),
        name="pick_columns",
    )(flip.reshape(1), rows)


def pick_rows(table, index):
    chosen = index[:, None] == jnp.arange(table.shape[0], dtype=jnp.int32)[None, :]
    return jnp.sum(jnp.where(chosen[:, :, None], table[None], 0.0), axis=1)


def held(value, beside):
    out = lax.optimization_barrier((value,) + tuple(beside))
    return out[0], out[1:]


def place_rows_body(plan, *refs):
    ins, out, held_ref, sems = refs[:-3], refs[-3], refs[-2], refs[-1]
    copies_in, copies_out = [], []
    for i, (source, low, rows, high) in enumerate(plan):
        middle = held_ref.at[high : high + rows, :]
        copies_in.append(
            pltpu.make_async_copy(ins[source].at[low : low + rows, :], middle, sems.at[0, i])
        )
        copies_out.append(
            pltpu.make_async_copy(middle, out.at[high : high + rows, :], sems.at[1, i])
        )
    for copy in copies_in:
        copy.start()
    for copy_in, copy_out in zip(copies_in, copies_out):
        copy_in.wait()
        copy_out.start()
    for copy in copies_out:
        copy.wait()


def place_rows(parts, plan):
    rows, cols = sum(entry[2] for entry in plan), parts[0].shape[1]
    size = rows * cols * parts[0].dtype.itemsize
    return pl.pallas_call(
        functools.partial(place_rows_body, plan),
        out_shape=jax.ShapeDtypeStruct((rows, cols), parts[0].dtype),
        in_specs=[pl.BlockSpec(memory_space=pl.ANY)] * len(parts),
        out_specs=pl.BlockSpec(memory_space=pl.ANY),
        scratch_shapes=[
            pltpu.VMEM((rows, cols), parts[0].dtype),
            pltpu.SemaphoreType.DMA((2, len(plan))),
        ],
        cost_estimate=pl.CostEstimate(flops=0, transcendentals=0, bytes_accessed=2 * size),
        name="place_rows",
    )(*parts)


def spread(piece, dp_size, split):
    rows = piece.shape[0]
    bits_x, bits_y = far_bits(dp_size)
    order = doubled(bits_x)
    parts, plans = (piece,), (bits_x,)
    if split:
        parts, plans = (piece[: rows // 2], piece[rows // 2 :]), (bits_x, bits_y)
    for step in range(len(bits_x)):
        parts = yield tuple(parts)
        got = [swap(part, "dp", bits[step], dp_size) for part, bits in zip(parts, plans)]
        if step + 1 < len(bits_x):
            parts = [jnp.concatenate(pair, axis=0) for pair in zip(parts, got)]
    got = yield tuple(got)
    if split:
        half, order_y, plan = rows // 2, doubled(bits_y), []
        count = len(order) // 2
        for i, at in enumerate(order):
            for side, places in enumerate((order, order_y)):
                j = places.index(at)
                source = side if j < count else 2 + side
                plan.append((source, (j % count) * half, half, (2 * i + side) * half))
        own = place_rows(list(parts) + list(got), plan)
    else:
        own = jnp.concatenate([parts[0], got[0]], axis=0)
    (own,) = yield (own,)
    yield own, swap(own, "dp", 1, dp_size)


def run(stages, values, count):
    for _ in range(count):
        values = stages.send(values)
    return values


def collect(own, odd, dp_size, split):
    bits_x, bits_y = far_bits(dp_size)
    order, count = doubled(bits_x), dp_size // 2
    odd = yield tuple(odd)
    got = [swap(part, "dp", 1, dp_size) for part in odd]
    stacks = [
        (a.reshape(count, -1, a.shape[1]), b.reshape(count, -1, a.shape[1]))
        for a, b in zip(own, got)
    ]
    rows = stacks[0][0].shape[1]

    def taken(which, low, high):
        cols = [
            jnp.concatenate([add(a[i, low:high], b[i, low:high]) for a, b in stacks], axis=1)
            for i in which
        ]
        return jnp.stack(cols)

    plans = [(bits_x, 0, rows)]
    if split:
        plans = [(bits_x, 0, rows // 2), (bits_y, rows // 2, rows)]
    keeps, sends = [], []
    half = count // 2
    for bits, low, high in plans:
        places = [order.index(at) for at in doubled(bits)]
        keeps.append(taken(places[:half], low, high))
        sends.append(taken(places[half:], low, high))
    for step in reversed(range(len(bits_x))):
        sends = yield tuple(sends)
        got = [swap(send, "dp", bits[step], dp_size) for send, (bits, _, _) in zip(sends, plans)]
        if step:
            cut = (1 << step) // 2
            sends = [add(keep[cut:], new[cut:]) for keep, new in zip(keeps, got)]
            keeps = [add(keep[:cut], new[:cut]) for keep, new in zip(keeps, got)]
        else:
            keeps = [add(keep, new)[0] for keep, new in zip(keeps, got)]
    yield (jnp.concatenate(keeps, axis=0),)


def seq_gather(shard, seq_size, earlier=None):
    out, earlier = [shard], list(earlier) if earlier else None
    for k in range(1, seq_size):
        sent = shard
        if earlier:
            sent, (earlier[k],) = held(shard, (earlier[k],))
        out.append(swap(sent, "seq", k, seq_size))
    return out, earlier


def seq_cuts(piece, seq_size, seq_at):
    rows = piece.shape[0] // seq_size
    return tuple(
        lax.dynamic_slice_in_dim(piece, jnp.bitwise_xor(seq_at, k) * rows, rows, 0)
        for k in range(seq_size)
    )


def dot(left, right):
    return jnp.dot(left, right, preferred_element_type=jnp.float32)


def dot_back(grad, weight):
    return jnp.einsum("rn,kn->rk", grad, weight, preferred_element_type=jnp.float32)


def dot_rows(rows, grad):
    return jnp.einsum("rk,rn->kn", rows, grad, preferred_element_type=jnp.float32)


def apply(rows, pair):
    half = rows.shape[1] // 2
    return dot(rows[:, :half], pair[0]) + dot(rows[:, half:], pair[1])


def apply_back(grad, pair, dtype=jnp.float32):
    return jnp.concatenate([dot_back(grad, part).astype(dtype) for part in pair], axis=1)


def weight_grads(rows, grad):
    half = rows.shape[1] // 2
    return [dot_rows(part, grad).astype(jnp.bfloat16) for part in (rows[:, :half], rows[:, half:])]


def seen(valid_ref, query_ref, key_ref):
    valid = valid_ref[0]
    query_at, query_seg, query_piece = (query_ref[:, i : i + 1] for i in range(3))
    key_at, key_seg, key_piece = (key_ref[i : i + 1, :] for i in range(3))
    together = (query_piece == key_piece) & (query_piece > 0)
    rule_ok = (query_seg == key_seg) & ((key_at <= query_at) | together)
    allowed = (key_at < valid) & ((query_at >= valid) | rule_ok)
    return jnp.where(allowed, 0.0, -1e30)


def one_head(rows, head):
    lane = lax.broadcasted_iota(jnp.int32, rows.shape, 1)
    return jnp.where(lane // HEAD_DIM == head, rows, jnp.zeros_like(rows))


def contract(left, right, dims):
    return lax.dot_general(left, right, (dims, ((), ())), preferred_element_type=jnp.float32)


def attend_body(valid_ref, query_ref, key_ref, q_ref, k_ref, v_ref, out_ref, lse_ref):
    hidden_keys = seen(valid_ref, query_ref, key_ref)
    columns = []
    for at in range(0, q_ref.shape[1], 128):
        pair = slice(at, at + 128)
        query, key, value = q_ref[:, pair] * HEAD_DIM ** (-0.5), k_ref[:, pair], v_ref[:, pair]
        outs = []
        for head in range(128 // HEAD_DIM):
            raw = contract(one_head(query, head), key, ((1,), (1,)))
            raw = raw + hidden_keys
            top = jnp.max(raw, axis=-1, keepdims=True)
            expo = jnp.exp(raw - top)
            total = jnp.sum(expo, axis=-1, keepdims=True)
            probs = (expo * (1.0 / total)).astype(jnp.bfloat16)
            outs.append(contract(probs, value, ((1,), (0,))))
            columns.append(top + jnp.log(total))
        lane = lax.broadcasted_iota(jnp.int32, outs[0].shape, 1)
        out_ref[:, pair] = jnp.where(lane < HEAD_DIM, outs[0], outs[1]).astype(out_ref.dtype)
    for i, column in enumerate(columns):
        lse_ref[:, i : i + 1] = column


def attend_back_body(
    valid_ref, query_ref, key_ref, lse_ref, q_ref, k_ref, v_ref, grad_ref, out_ref, sum_ref
):
    step, group = pl.program_id(0), q_ref.shape[1]
    rows = q_ref.shape[0]

    @pl.when(step == 0)
    def _():
        sum_ref[...] = jnp.zeros_like(sum_ref)

    hidden_keys = seen(valid_ref, query_ref, key_ref)
    at_rows = pl.ds(pl.multiple_of(step * rows, rows), rows)
    scale = HEAD_DIM ** (-0.5)
    for at in range(0, group, 128):
        pair = slice(at, at + 128)
        query, key, value, grad = q_ref[:, pair] * scale, k_ref[:, pair], v_ref[:, pair], grad_ref[:, pair]
        grad_query = grad_key = grad_value = 0.0
        for head in range(128 // HEAD_DIM):
            column = at // HEAD_DIM + head
            own_query, own_grad = one_head(query, head), one_head(grad, head)
            raw = contract(own_query, key, ((1,), (1,))) + hidden_keys
            probs = jnp.exp(raw - lse_ref[:, column : column + 1])
            grad_probs = contract(own_grad, value, ((1,), (1,)))
            inner = jnp.sum(probs * grad_probs, axis=-1, keepdims=True)
            grad_scores = (probs * (grad_probs - inner)).astype(jnp.bfloat16)
            grad_value += contract(probs.astype(jnp.bfloat16), own_grad, ((0,), (0,)))
            grad_key += contract(grad_scores, own_query, ((0,), (0,)))
            grad_query += contract(grad_scores, one_head(key, head), ((1,), (0,)))
        out_ref[at_rows, pair] = (grad_query * scale).astype(out_ref.dtype)
        sum_ref[:, pair] += grad_key
        sum_ref[:, group + at : group + at + 128] += grad_value

    @pl.when(step == pl.num_programs(0) - 1)
    def _():
        out_ref[:, group : 2 * group] = sum_ref[:, :group].astype(out_ref.dtype)
        out_ref[:, 2 * group :] = sum_ref[:, group:].astype(out_ref.dtype)


def attention_specs(length, group, block):
    whole = lambda column: pl.BlockSpec((length, group), lambda i: (0, column))
    return [
        pl.BlockSpec(memory_space=pltpu.SMEM),
        pl.BlockSpec((block, 3), lambda i: (i, 0)),
        pl.BlockSpec((3, length), lambda i: (0, 0)),
    ], [pl.BlockSpec((block, group), lambda i: (i, 0)), whole(1), whole(2)]


def attend(valid, query_info, key_info, qkv_rows, block=256):
    length, group = qkv_rows.shape[0], qkv_rows.shape[1] // 3
    heads = group // HEAD_DIM
    info_specs, qkv_specs = attention_specs(length, group, block)
    work = heads * length * length
    return pl.pallas_call(
        attend_body,
        grid=(length // block,),
        in_specs=info_specs + qkv_specs,
        out_specs=[
            pl.BlockSpec((block, group), lambda i: (i, 0)),
            pl.BlockSpec((block, heads), lambda i: (i, 0)),
        ],
        out_shape=[
            jax.ShapeDtypeStruct((length, group), jnp.bfloat16),
            jax.ShapeDtypeStruct((length, heads), jnp.float32),
        ],
        cost_estimate=pl.CostEstimate(
            flops=16 * work * HEAD_DIM, transcendentals=work, bytes_accessed=32 * length * group
        ),
        name="attend",
    )(valid, query_info, key_info, qkv_rows, qkv_rows, qkv_rows)


def attend_back(valid, query_info, key_info, lse, qkv_rows, grad_rows, block=256):
    length, group = grad_rows.shape
    heads = group // HEAD_DIM
    info_specs, qkv_specs = attention_specs(length, group, block)
    work = heads * length * length
    return pl.pallas_call(
        attend_back_body,
        grid=(length // block,),
        in_specs=info_specs
        + [pl.BlockSpec((block, heads), lambda i: (i, 0))]
        + qkv_specs
        + [pl.BlockSpec((block, group), lambda i: (i, 0))],
        out_specs=pl.BlockSpec((length, 3 * group), lambda i: (0, 0)),
        out_shape=jax.ShapeDtypeStruct((length, 3 * group), jnp.bfloat16),
        scratch_shapes=[pltpu.VMEM((length, 2 * group), jnp.float32)],
        cost_estimate=pl.CostEstimate(
            flops=40 * work * HEAD_DIM, transcendentals=work, bytes_accessed=64 * length * group
        ),
        name="attend_back",
    )(valid, query_info, key_info, lse, qkv_rows, qkv_rows, qkv_rows, grad_rows)


def per_device(
    tokens,
    cotangent,
    valid_length,
    segment_ids,
    piece_starts,
    norm1_gain,
    norm1_bias,
    qkv_weight,
    qv_bias,
    out_weight,
    out_bias,
    norm2_gain,
    norm2_bias,
    up_weight,
    up_bias,
    down_weight,
    down_bias,
):
    f32, bf16 = jnp.float32, jnp.bfloat16
    _, local_len, width = tokens.shape
    dp_size, seq_size = lax.axis_size("dp"), lax.axis_size("seq")
    dp_at, seq_at = lax.axis_index("dp"), lax.axis_index("seq")
    devices = dp_size * seq_size
    group = width // seq_size

    half_order = doubled(far_bits(dp_size)[0])
    full = half_order + [at ^ 1 for at in half_order]
    back = [full.index(at) for at in range(dp_size)]
    place_in_x = lambda block: sum(
        jnp.where(jnp.bitwise_and(block, 1 << i) > 0, back[1 << i], 0)
        for i in range(dp_size.bit_length() - 1)
    )
    to_x, from_x = (full, dp_at), (back, place_in_x(dp_at))
    in_groups = jnp.bitwise_xor(dp_at, seq_at * (dp_size // seq_size))
    groups_to_x, x_to_groups = (full, in_groups), (back, place_in_x(in_groups))
    index_of = lambda rule: jnp.bitwise_xor(jnp.array(rule[0], jnp.int32), rule[1])

    vectors = (norm1_gain, norm1_bias, qv_bias, out_bias, norm2_gain, norm2_bias, up_bias, down_bias)
    widths = [v.shape[0] for v in vectors]
    rows_one = qkv_weight.shape[0]
    slots = len(vectors) + 1
    in_row = -(-slots // rows_one)
    slot = 128 // in_row
    vec_rows = -(-slots // in_row)

    def slotted(parts):
        rows = []
        for at in range(0, len(parts), in_row):
            row = [
                jnp.pad(v, [(0, 0)] * (v.ndim - 1) + [(0, slot - v.shape[-1])])
                for v in parts[at : at + in_row]
            ]
            row = jnp.concatenate(row, axis=-1) if in_row > 1 else row[0]
            rows.append(jnp.pad(row, [(0, 0)] * (row.ndim - 1) + [(0, 128 - row.shape[-1])]))
        return jnp.stack(rows, axis=-2)

    def whole_rows(rows):
        return jnp.pad(rows, [(0, 0)] * (rows.ndim - 2) + [(0, rows_one - rows.shape[-2]), (0, 0)])

    def from_slot(table, which):
        row, low = which // in_row, (which % in_row) * slot
        size = widths[which] if which < len(widths) else 6
        return table[..., row, low : low + size]

    vec_block = whole_rows(slotted(vectors))
    qkv_split = qkv_weight.reshape(rows_one, 3, seq_size, group)

    def qkv_part(k):
        mine = lax.dynamic_index_in_dim(qkv_split, jnp.bitwise_xor(seq_at, k), 2, keepdims=False)
        return jnp.concatenate([mine.reshape(rows_one, 3 * group), vec_block], axis=1)

    first = [qkv_part(0)] + [swap(qkv_part(k), "seq", k, seq_size) for k in range(1, seq_size)]
    own_x = pick_columns(tokens[0], *to_x)
    second, _ = seq_gather(jnp.concatenate([out_weight, up_weight], axis=1), seq_size)
    token_blocks = [own_x]
    for k in range(1, seq_size):
        sent, (first[k], second[k]) = held(own_x, (first[k], second[k]))
        token_blocks.append(swap(sent, "seq", k, seq_size))
    far = dp_size.bit_length() - 2
    stacked = lambda blocks: jnp.concatenate(by_place(blocks, seq_at), axis=0)
    one_parts = spread(stacked(first), dp_size, False)
    one_pair = run(one_parts, next(one_parts), far + 2)
    two_parts = spread(stacked(second), dp_size, True)
    two_sends = run(two_parts, next(two_parts), far - 1)
    token_blocks[0], beside = held(token_blocks[0], tuple(token_blocks[1:]) + two_sends)
    token_blocks = token_blocks[:1] + list(beside[: seq_size - 1])
    got = two_parts.send(beside[seq_size - 1 :])
    third, token_blocks = seq_gather(down_weight, seq_size, token_blocks)
    qkv_pair = [part[:, : 3 * group] for part in one_pair]

    vec_x = jnp.concatenate([part[:, 3 * group :] for part in one_pair], axis=0).astype(f32)
    vec_x = vec_x.reshape(dp_size, seq_size, rows_one, 128)[:, :, :vec_rows]
    vec_n = pick_rows(vec_x.reshape(dp_size, -1), index_of(from_x)).reshape(vec_x.shape)

    field = lambda table, which: from_slot(table, which).reshape(-1)
    gain_one, shift_one, gain_two, shift_two = [field(vec_x, i) for i in (0, 1, 4, 5)]
    qv_full, out_shift, up_shift, down_shift = [field(vec_n, i) for i in (2, 3, 6, 7)]

    starts = [jnp.bitwise_xor(seq_at, k) * local_len for k in range(seq_size)]
    step = jnp.arange(local_len, dtype=jnp.int32)
    place = jnp.concatenate([at + step for at in starts])
    segments = jnp.concatenate(
        [lax.dynamic_slice_in_dim(segment_ids, at, local_len, 1) for at in starts], axis=1
    )
    pieces = piece_labels(place[None, :], piece_starts)
    key_info = jnp.concatenate([place[None], segments, pieces], axis=0)
    query_info = key_info.T
    live_rows = (starts[0] + step < valid_length[0]).astype(f32)[:, None]

    all_x = jnp.concatenate(token_blocks, axis=0).astype(f32)
    normed_one, unit_all, _ = layer_norm_parts(all_x, gain_one, shift_one)
    normed_one = normed_one.astype(bf16)
    half_bias = qv_full.reshape(2, seq_size, group)
    half_bias = lax.dynamic_index_in_dim(half_bias, seq_at, 1, keepdims=False)
    qkv_shift = jnp.concatenate([half_bias[0], jnp.zeros((group,), f32), half_bias[1]])
    qkv_rows = (apply(normed_one, qkv_pair) + qkv_shift).astype(bf16)
    attended_rows, lse_all = attend(valid_length, query_info, key_info, qkv_rows)
    attended_rows, beside = held(attended_rows, tuple(third) + tuple(got))
    third, got = beside[:-2], beside[-2:]
    cut_rows = lambda rows, k: rows[k * local_len : (k + 1) * local_len]
    attended = [cut_rows(attended_rows, 0)] + [
        swap(cut_rows(attended_rows, k), "seq", k, seq_size) for k in range(1, seq_size)
    ]
    own, (piece,) = held(two_parts.send(got)[0], (stacked(third),))
    two_pair = two_parts.send((own,))
    out_pair = [part[:, :width] for part in two_pair]
    up_pair = [part[:, width:] for part in two_pair]
    down_parts = spread(piece, dp_size, True)
    down_sends = run(down_parts, next(down_parts), far - 1)

    attended, down_sends = held(jnp.concatenate(attended, axis=1), down_sends)
    got = down_parts.send(down_sends)
    attended = pick_columns(attended, *groups_to_x)
    branch = apply(attended, out_pair) + out_shift
    tokens_f = tokens[0].astype(f32)
    middle = tokens_f + branch
    middle_x = pick_columns(middle, *to_x)
    normed_two, unit_two, inverse_two = layer_norm_parts(middle_x, gain_two, shift_two)
    normed_two = normed_two.astype(bf16)
    hidden = pick_columns(apply(normed_two, up_pair) + up_shift, *to_x)
    hidden, got = held(hidden, got)
    down_pair = run(down_parts, got, 2)
    gated = gelu_parts(hidden)[0].astype(bf16)
    grad_out = cotangent[0] * live_rows.astype(bf16)
    down_grads = weight_grads(gated, grad_out)
    down_sum = collect([down_grads[0]], [down_grads[1]], dp_size, True)
    grad_out_later, sends = held(grad_out, next(down_sum))
    down_sends = down_sum.send(sends)
    hidden_later, down_sends = held(hidden, down_sends)
    down_sends = down_sum.send(down_sends)
    grad_hidden = apply_back(grad_out_later, down_pair) * gelu_parts(hidden_later)[1]
    grad_hidden = pick_columns(grad_hidden.astype(bf16), *from_x)
    up_grads = weight_grads(normed_two, grad_hidden)
    up_sum = collect([up_grads[0]], [up_grads[1]], dp_size, True)
    grad_hidden_later, sends = held(grad_hidden, next(up_sum))
    up_sends = up_sum.send(sends)
    grad_normed_two = apply_back(grad_hidden_later, up_pair)
    grad_mid_norm, grad_norm2_gain, grad_norm2_bias = layer_norm_back(
        grad_normed_two, unit_two, inverse_two, gain_two
    )
    grad_mid_norm = pick_columns(grad_mid_norm, *from_x)
    grad_middle = grad_out.astype(f32) + grad_mid_norm
    grad_branch = grad_middle.astype(bf16)
    out_grads = weight_grads(attended, grad_branch)
    grad_attended = pick_columns(apply_back(grad_branch, out_pair, bf16), *x_to_groups)
    grad_attended, (gated_later,) = held(grad_attended, (gated,))
    mlp_out = apply(gated_later, down_pair) + down_shift
    result = middle + mlp_out
    output = result.astype(bf16)[None]
    squares = [
        jnp.sum(live_rows * entry * entry)
        for entry in (tokens_f, branch, middle, mlp_out, result)
    ]
    slots_at = jnp.arange(6, dtype=jnp.int32)
    counted = sum(
        jnp.where(slots_at == i, value, 0.0)
        for i, value in enumerate(squares + [jnp.sum(live_rows)])
    )
    cut_cols = lambda rows, k: rows[:, k * group : (k + 1) * group]
    grad_heads = jnp.concatenate(
        [cut_cols(grad_attended, 0)]
        + [swap(cut_cols(grad_attended, k), "seq", k, seq_size) for k in range(1, seq_size)],
        axis=0,
    )
    grad_heads, sends = held(grad_heads, tuple(down_sends) + tuple(up_sends))
    down_cuts = seq_cuts(run(down_sum, sends[:2], far - 1)[0], seq_size, seq_at)
    up_sends = run(up_sum, sends[2:], far - 1)
    grad_qkv = attend_back(valid_length, query_info, key_info, lse_all, qkv_rows, grad_heads)
    grad_qkv, down_cuts = held(grad_qkv, down_cuts)
    down_blocks = [down_cuts[0]]
    down_blocks += [swap(down_cuts[k], "seq", k, seq_size) for k in range(1, seq_size)]
    part_normed = apply_back(grad_qkv, qkv_pair)
    grad_norm1_gain = jnp.sum(part_normed * unit_all, axis=0)
    grad_norm1_bias = jnp.sum(part_normed, axis=0)
    part_normed = part_normed.astype(bf16)
    column_sums = jnp.sum(grad_qkv.astype(f32), axis=0).reshape(3, 1, group)
    grad_qv_bias = lax.dynamic_update_slice(
        jnp.zeros((2, seq_size, group), f32),
        jnp.concatenate([column_sums[:1], column_sums[2:]], axis=0),
        (0, seq_at, 0),
    )
    grad_out_bias = jnp.sum(grad_branch.astype(f32), axis=0)
    grad_up_bias = jnp.sum(grad_hidden.astype(f32), axis=0)
    grad_down_bias = jnp.sum(grad_out.astype(f32), axis=0)
    by_device = lambda v: v.reshape(dp_size, seq_size, -1)
    plain = [by_device(v) for v in (grad_qv_bias, grad_out_bias, grad_up_bias, grad_down_bias)]
    moved = [by_device(v) for v in (grad_norm1_gain, grad_norm1_bias, grad_norm2_gain, grad_norm2_bias)]
    spare = [jnp.zeros((dp_size, seq_size, 1), f32)] * 2
    counts = jnp.broadcast_to(counted, (dp_size, seq_size, 6))
    plain_x = slotted(spare + plain[:2] + spare + plain[2:] + [counts])
    plain_x = pick_rows(plain_x.reshape(dp_size, -1), index_of(to_x)).reshape(plain_x.shape)
    spare = spare[:1] * 2
    vec_grads = plain_x + slotted(moved[:2] + spare + moved[2:] + spare + spare[:1])
    vec_grads = whole_rows(vec_grads.astype(bf16)).reshape(2, -1, 128)
    qkv_grads = weight_grads(normed_one, grad_qkv)
    one_sum = collect(
        [qkv_grads[0], vec_grads[0], out_grads[0]],
        [qkv_grads[1], vec_grads[1], out_grads[1]],
        dp_size,
        False,
    )
    odd = next(one_sum)
    part_normed, beside = held(
        part_normed, (odd[0], odd[2]) + tuple(up_sends) + tuple(down_blocks)
    )
    up_cuts = seq_cuts(up_sum.send(beside[2:4])[0], seq_size, seq_at)
    down_blocks = beside[4:]
    sends = run(one_sum, (beside[0], odd[1], beside[1]), far + 1)
    one_cuts = seq_cuts(sends[0], seq_size, seq_at)
    parts = [cut_rows(part_normed, 0)]
    parts += [swap(cut_rows(part_normed, k), "seq", k, seq_size) for k in range(1, seq_size)]
    parts[1], beside = held(parts[1], one_cuts + up_cuts)
    one_cuts, up_cuts = beside[:seq_size], beside[seq_size:]
    up_blocks = [up_cuts[0]] + [swap(up_cuts[k], "seq", k, seq_size) for k in range(1, seq_size)]
    one_blocks = [one_cuts[0]]
    one_blocks += [swap(one_cuts[k], "seq", k, seq_size) for k in range(1, seq_size)]
    grad_normed_one = sum(part.astype(f32) for part in parts)
    unit_one, inverse_one = layer_norm_parts(own_x.astype(f32), gain_one, shift_one)[1:]
    grad_in_norm = layer_norm_back(grad_normed_one, unit_one, inverse_one, gain_one)[0]
    tokens_grad = (grad_middle + pick_columns(grad_in_norm, *from_x)).astype(bf16)[None]
    tokens_grad, up_blocks = held(tokens_grad, up_blocks)
    up_grad = sum(block.astype(f32) for block in up_blocks)
    down_grad = sum(block.astype(f32) for block in down_blocks)
    one_blocks = [block.astype(f32) for block in one_blocks]
    qkv_grad = jnp.stack(
        [part.reshape(rows_one, 3, group) for part in by_place([b[:, : 3 * group] for b in one_blocks], seq_at)],
        axis=2,
    ).reshape(rows_one, 3 * width)
    rest_sum = sum(block[:, 3 * group :] for block in one_blocks)
    vec_sum, out_grad = rest_sum[:, :128], rest_sum[:, 128:]
    n1g, n1b, qvb, ob, n2g, n2b, ub, db, counted = [from_slot(vec_sum, i) for i in range(slots)]
    residual_rms = jnp.sqrt(counted[:5] / (counted[5] * width))

    return (
        output,
        tokens_grad,
        n1g,
        n1b,
        qkv_grad,
        qvb,
        out_grad,
        ob,
        n2g,
        n2b,
        up_grad,
        ub,
        down_grad,
        db,
        residual_rms,
    )


def solution(mesh):
    return jax.shard_map(
        per_device,
        mesh=mesh,
        in_specs=(
            P("dp", "seq", None),
            P("dp", "seq", None),
            P("dp"),
            P("dp", None),
            P("dp", None),
            P(("dp", "seq")),
            P(("dp", "seq")),
            P(("dp", "seq"), None),
            P(("dp", "seq")),
            P(("dp", "seq"), None),
            P(("dp", "seq")),
            P(("dp", "seq")),
            P(("dp", "seq")),
            P(("dp", "seq"), None),
            P(("dp", "seq")),
            P(("dp", "seq"), None),
            P(("dp", "seq")),
        ),
        out_specs=(
            P("dp", "seq", None),
            P("dp", "seq", None),
            P(("dp", "seq")),
            P(("dp", "seq")),
            P(("dp", "seq"), None),
            P(("dp", "seq")),
            P(("dp", "seq"), None),
            P(("dp", "seq")),
            P(("dp", "seq")),
            P(("dp", "seq")),
            P(("dp", "seq"), None),
            P(("dp", "seq")),
            P(("dp", "seq"), None),
            P(("dp", "seq")),
            P(),
        ),
        check_vma=False,
    )
```
